128 devices in a mesh: tm: 32 (over z, y, core), obs: 4 (over x).
Axes of the slice: x: 4, y: 4, z: 4, core: 2. Of those that a mesh axis runs over, the one named last changes fastest.
Arguments:
- records: bfloat16 [524288, 512], P(('tm', 'obs')), may hold values from -0.25 to 0.25
- obs_values: bfloat16 [524288], P(('tm', 'obs')), may hold values from -18 to 18
- block_day: int32 [4096], P(('tm', 'obs')), may hold values from 0 to 1
- block_count: int32 [4096], P(('tm', 'obs')), may hold values from 1 to 128
- propagator_matrix: float32 [512, 512], replicated, may hold values from -1 to 1
- analysis_cov: float32 [512, 512], replicated, may hold values from -0.05 to 0.1, as said below
- unattenuated_multiplier: float32 [512, 512], P('obs'), may hold values from -0.3 to 1
- damping: float32 [64, 512], P('tm'), may hold values from 0 to 1
- prior_mean: float32 [512], P('obs'), may hold values from -6 to 6
Outputs:
- filtered: float32 [64, 512], P('tm', 'obs')
- smoothed: float32 [64, 512], P('tm', 'obs')
The draws below stay inside these ranges and needn't reach their ends.
Inputs may be any that keep to these rules, and one draw needn't show every extreme that they name: `analysis_cov`: Symmetric.
All inputs are finite; a program needn't handle non-finite values.
Results may differ from the reference program's by a relative error of at most 0.0003.
Values may be sent and summed in bfloat16 or wider, within the bound.
A program may use at most 192 MiB of HBM per device.

```python
import math
import jax
import jax.numpy as jnp
from jax import lax

S = 512
BLOCK = 128
DAYS_DEV = 2
WINDOW_DAYS = 64
BLOCKS = 4096
N_TM = 32
N_OBS = 4


def draw_propagator_matrix(key, part):
    random_keys = jax.random.split(key, 2)
    noise = jax.random.normal(random_keys[0], (S, S), jnp.float32) * (0.02 / math.sqrt(S))
    diagonal = jax.random.uniform(random_keys[1], (S,), jnp.float32, 0.93, 1.0)
    return jnp.diag(diagonal) + (noise - noise.T)


def draw_analysis_cov(key, part):
    random_keys = jax.random.split(key, 2)
    lowest = 0.25 / WINDOW_DAYS
    variance = jnp.exp(jax.random.uniform(random_keys[0], (S,), jnp.float32, math.log(lowest), math.log(0.05)))
    noise = jax.random.normal(random_keys[1], (S, S), jnp.float32)
    mirror = 0.5 * (noise + noise.T)
    root = jnp.sqrt(variance)
    return jnp.diag(variance) + 0.3 * root[:, None] * root[None, :] * mirror / math.sqrt(S)


def draw_unattenuated_multiplier(key, part):
    random_keys = jax.random.split(key, 2)
    lowest, maximal_accuracy = (0.5 / WINDOW_DAYS, 1.0 / 30.0)
    rates = jnp.exp(jax.random.uniform(random_keys[0], (S,), jnp.float32, math.log(lowest), math.log(maximal_accuracy)))
    noise = jax.random.normal(random_keys[1], (S, S), jnp.float32) * (0.02 / math.sqrt(S))
    return jnp.diag(jnp.exp(-rates)) + (noise - noise.T)


def draw_damping(key, part):
    random_keys = jax.random.split(key, 4)
    spans = WINDOW_DAYS // DAYS_DEV
    lowest, maximal_accuracy = (0.25 / WINDOW_DAYS, 1.0 / 30.0)
    rates = jnp.exp(jax.random.uniform(random_keys[0], (1, 1, S), jnp.float32, math.log(lowest), math.log(maximal_accuracy)))
    spread = jnp.exp(jax.random.uniform(random_keys[1], (spans, 1, S), jnp.float32, math.log(0.5), 0.0))
    decay_factor = jnp.broadcast_to(rates * spread, (spans, DAYS_DEV, S)).reshape(WINDOW_DAYS, S)
    sudden_shock = jax.random.uniform(random_keys[2], (WINDOW_DAYS, 1), jnp.float32) < 3.0 / WINDOW_DAYS
    dropped_rows = jax.random.uniform(random_keys[3], (WINDOW_DAYS, S), jnp.float32, 0.5, 0.8)
    return jnp.exp(-decay_factor) * jnp.where(sudden_shock, dropped_rows, 1.0)


def set_ends(array, own_key, least, top_value):
    extent = array.shape
    index_at = [jax.random.randint(jax.random.fold_in(own_key, axis), (), 0, extent[axis]) for axis in range(len(extent))]
    array = array.at[tuple(index_at)].set(least)
    longest = extent.index(max(extent))
    index_at[longest] = (index_at[longest] + 1) % extent[longest]
    return array.at[tuple(index_at)].set(top_value)


def block_levels(key, dims, shards, low, top_value):
    def one(dim, blocks):
        steps = jax.random.uniform(jax.random.fold_in(jax.random.fold_in(key, 6), dim), (blocks,), jnp.float32, low / len(shards), top_value / len(shards))
        return jnp.repeat(jnp.exp(steps), dims[dim] // blocks).reshape((-1,) + (1,) * (len(dims) - dim - 1))

    level = one(*shards[0])
    for cut in shards[1:]:
        level = level * one(*cut)
    return level


def scatter_about(key, extent, scale, reach, cuts=(), kind=jnp.bfloat16):
    loudness = block_levels(key, extent, cuts, -0.22, 0.18) if cuts else 1.0
    result = jax.random.normal(key, extent, jnp.float32) * scale * loudness
    return jnp.minimum(jnp.maximum(result, -reach), reach).astype(kind)


def setup_inputs(seed: int = 0) -> dict:
    key_list = jax.random.split(jax.random.key(seed), 10)
    return {
        "records": scatter_about(key_list[0], (BLOCKS * BLOCK, S), S ** -0.5, 0.25, ((0, 128),)),
        "obs_values": scatter_about(key_list[1], (BLOCKS * BLOCK,), 3.0, 18.0, ((0, 128),)),
        "block_day": set_ends(jax.random.randint(key_list[2], (BLOCKS,), 0, DAYS_DEV), jax.random.fold_in(key_list[2], 1), 0, DAYS_DEV - 1).astype(jnp.int32),
        "block_count": set_ends(jax.random.randint(key_list[3], (BLOCKS,), 1, BLOCK + 1), jax.random.fold_in(key_list[3], 1), 1, BLOCK).astype(jnp.int32),
        "propagator_matrix": draw_propagator_matrix(jax.random.fold_in(key_list[9], 71), 0),
        "analysis_cov": draw_analysis_cov(jax.random.fold_in(key_list[9], 71), 0),
        "unattenuated_multiplier": draw_unattenuated_multiplier(jax.random.fold_in(key_list[9], 71), 0),
        "damping": draw_damping(jax.random.fold_in(key_list[9], 71), 0),
        "prior_mean": scatter_about(key_list[8], (S,), 1.0, 6.0, ((0, 4),), jnp.float32),
    }


def day_grams(rows_all, values_all, days_of_block, counts_of_block, day_total):
    maximal_accuracy = lax.Precision.HIGHEST
    block_total = days_of_block.shape[0]
    slot_total = rows_all.shape[0] // block_total
    width = rows_all.shape[1]
    group = math.gcd(block_total, 8)
    slot_index = lax.broadcasted_iota(jnp.int32, (block_total, slot_total), 1)
    valid_mask = slot_index < counts_of_block[:, None]
    held_rows = jnp.where(valid_mask[:, :, None], rows_all.reshape(block_total, slot_total, width).astype(jnp.float32), 0.0)
    held_values = jnp.where(valid_mask, values_all.reshape(block_total, slot_total).astype(jnp.float32), 0.0)
    day_mark = (days_of_block[:, None] == lax.broadcasted_iota(jnp.int32, (block_total, day_total), 1)).astype(jnp.float32)
    block_info = jnp.einsum('bk,bks->bs', held_values, held_rows, precision=maximal_accuracy)
    info = jnp.einsum('bd,bs->ds', day_mark, block_info, precision=maximal_accuracy)
    grouped_rows = held_rows.reshape(block_total // group, group, slot_total, width)
    grouped_mark = day_mark.reshape(block_total // group, group, day_total)

    def add_group(running, pieces):
        block_part, mark_part = pieces
        gram_blocks = jnp.einsum('bks,bkt->bst', block_part, block_part, precision=maximal_accuracy)
        return running + jnp.einsum('bd,bst->dst', mark_part, gram_blocks, precision=maximal_accuracy), None

    omega, _ = lax.scan(add_group, jnp.zeros((day_total, width, width), jnp.float32), (grouped_rows, grouped_mark))
    return omega, info


def reference(records, obs_values, block_day, block_count, propagator_matrix, analysis_cov, unattenuated_multiplier, damping, prior_mean):
    maximal_accuracy = lax.Precision.HIGHEST
    owners = N_TM * N_OBS
    span_rows = jnp.swapaxes(records.reshape(owners, N_TM, BLOCK, S), 0, 1)
    span_values = jnp.swapaxes(obs_values.reshape(owners, N_TM, BLOCK), 0, 1)
    span_days = jnp.swapaxes(block_day.reshape(owners, N_TM), 0, 1)
    span_counts = jnp.swapaxes(block_count.reshape(owners, N_TM), 0, 1)

    def per_span(pieces):
        rows_part, values_part, days_part, counts_part = pieces
        return day_grams(rows_part.reshape(owners * BLOCK, S), values_part.reshape(owners * BLOCK), days_part, counts_part, DAYS_DEV)

    omega, info = lax.map(per_span, (span_rows, span_values, span_days, span_counts))
    omega = omega.reshape(WINDOW_DAYS, S, S)
    info = info.reshape(WINDOW_DAYS, S)

    def forward(state, pieces):
        omega_day, info_day, attenuated_date = pieces
        moved = attenuated_date * jnp.dot(propagator_matrix, state, precision=maximal_accuracy)
        updated_vector = moved - jnp.dot(analysis_cov, jnp.dot(omega_day, moved, precision=maximal_accuracy) - info_day, precision=maximal_accuracy)
        return updated_vector, updated_vector

    _, filtered = lax.scan(forward, prior_mean, (omega, info, damping))
    attenuated_successor = jnp.concatenate([damping[1:], jnp.zeros((1, S), jnp.float32)], 0)

    def backward(subsequent_dates, pieces):
        assimilated_date, attenuated_date = pieces
        predicted_vector = attenuated_date * jnp.dot(propagator_matrix, assimilated_date, precision=maximal_accuracy)
        updated_vector = assimilated_date + jnp.dot(unattenuated_multiplier, attenuated_date * (subsequent_dates - predicted_vector), precision=maximal_accuracy)
        return updated_vector, updated_vector

    _, smoothed = lax.scan(backward, jnp.zeros((S,), jnp.float32), (filtered, attenuated_successor), reverse=True)
    return filtered, smoothed
```

```python
import jax
import jax.numpy as jnp
from jax import lax
from jax.experimental import pallas as pl
from jax.experimental.pallas import tpu as pltpu
from jax.sharding import PartitionSpec as P

MESH = pl.DeviceIdType.MESH
F32 = jnp.float32
BF16 = jnp.bfloat16
HIGH = lax.Precision.HIGHEST
S = 512


def row_place(r):
    g, i = r // 4, r % 4
    im = i % 3
    return (2 * (g % 2) + im * (im + 1) // 2) % 4, (g + i // 3) % 4


def place_row(y, z):
    phi = (y + 2 * z) % 4
    i = phi + (phi // 2) * (5 - 2 * phi)
    g = (z - i // 3 + 4) % 4
    return g, i


def row_times(ref, row):
    parts = []
    for k in range(0, S, 128):
        block = ref[k:k + 128, :]
        total = block[:, 0:128] * row[:, 0:128]
        for n in range(128, S, 128):
            total = total + block[:, n:n + 128] * row[:, n:n + 128]
        parts.append(jnp.sum(total, axis=1, keepdims=True))
    return jnp.concatenate(parts, axis=0)


def col_times(ref, col):
    total = ref[0:32, :] * col[0:32, :]
    for k in range(32, S, 32):
        total = total + ref[k:k + 32, :] * col[k:k + 32, :]
    return jnp.sum(total, axis=0, keepdims=True)


def to_row(col):
    return jnp.broadcast_to(col, (S, 128)).T[0:1, :]


def dot(a, b):
    return jnp.dot(a, b, precision=HIGH, preferred_element_type=F32)


def dot_nt(a, b):
    return lax.dot_general(a, b, (((1,), (1,)), ((), ())), precision=HIGH, preferred_element_type=F32)


def kernel(rec, meta, prop, cov, kslab, damp, prior, filt_out, smooth_out,
           land, mland, lhs, acc, r1, hs, r2, fh, r3, ri, om, wide, slab, slab_t, brow, maps, brows, kfull, k_t,
           dsrc, dl, psrc, pr, hop_src, hop_in, start_src, start_in, msg, mail,
           s_rec, r_rec, s_meta, r_meta, s_k, r_k, s_d, r_d, s_p, r_p, s_1, r_1, s_i, r_i, s_2, r_2, s_3, r_3,
           s_a, r_a, s_b, r_b, s_h, r_h, s_s, r_s, s_m, r_m, l_rec, l_meta):
    tm, x = lax.axis_index("tm"), lax.axis_index("obs")
    z, y, core = tm // 8, (tm // 2) % 4, tm % 2
    q, xi = x // 2, x % 2
    g, i_row = place_row(y, z)
    e_me = 2 * i_row + q
    c_me = 8 * g + e_me
    j = 2 * xi + core
    lead_tm = g * 8 + (2 * (g % 2)) * 2
    is_lead = jnp.logical_and(tm == lead_tm, x == 1)
    sib = tm + 1 - 2 * core
    xp = x + 1 - 2 * xi

    def remote(src, dst, ss, rs, dev):
        return pltpu.make_async_remote_copy(src_ref=src, dst_ref=dst, send_sem=ss, recv_sem=rs, device_id=dev,
                                            device_id_type=MESH)

    me = tm * 4 + x
    barrier = pltpu.get_barrier_semaphore()

    def greet(n, carry):
        other = (me + n) % 128
        pl.semaphore_signal(barrier, 1, device_id=(other // 4, other % 4), device_id_type=MESH)
        return carry

    lax.fori_loop(1, 128, greet, 0)
    pl.semaphore_wait(barrier, 127)

    def offset(m):
        return 1 + ((m - 1) * 11 + core * 15) % 31

    def record_copies(m):
        o = offset(m)
        dq, ty, tz = o // 16, (y + (o // 4) % 4) % 4, (z + o % 4) % 4
        tq = (q + dq) % 2
        tx = x + dq * (3 - 2 * x)
        tg, ti = place_row(ty, tz)
        c = 8 * tg + 2 * ti + tq
        dev = (tz * 8 + ty * 2 + core, tx)
        return (
            remote(rec.at[pl.ds(pl.multiple_of(c * 128, 128), 128)],
                   land.at[m // 2, pl.ds(pl.multiple_of((m % 2) * 128, 128), 128)], s_rec.at[m], r_rec.at[m], dev),
            remote(meta.at[c], mland.at[m], s_meta.at[m], r_meta.at[m], dev),
        )

    own_rec = pltpu.make_async_copy(rec.at[pl.ds(pl.multiple_of(c_me * 128, 128), 128)],
                                    land.at[0, pl.ds(0, 128)], l_rec)
    own_rec.start()
    own_meta = pltpu.make_async_copy(meta.at[c_me], mland.at[0], l_meta)
    own_meta.start()

    def send_record(m, carry):
        a, b = record_copies(m)
        b.start()
        a.start()
        return carry

    dsrc[...] = jnp.zeros_like(dsrc)
    dsrc[0:2, :] = damp[...]
    dr_y, dr_z = row_place(tm // 2)
    d_tm, d_x = dr_z * 8 + dr_y * 2 + x % 2, 2 * (tm % 2) + x // 2
    d_self = jnp.logical_and(d_tm == tm, d_x == x)
    d_copy = remote(dsrc, dl, s_d.at[0], r_d.at[0], (d_tm, d_x))

    @pl.when(d_self)
    def _():
        dl[...] = dsrc[...]

    @pl.when(jnp.logical_not(d_self))
    def _():
        d_copy.start()

    psrc[...] = jnp.broadcast_to(prior[...], (8, 128))
    p_copy = remote(psrc, pr.at[x], s_p.at[0], r_p.at[x], (0, 1))
    p_send = jnp.logical_and(tm == 0, x != 1)

    @pl.when(p_send)
    def _():
        p_copy.start()

    @pl.when(jnp.logical_and(tm == 0, x == 1))
    def _():
        pr[1] = psrc[...]

    lax.fori_loop(1, 32, send_record, 0)

    def gain_copy(n):
        return remote(kslab, kfull.at[pl.ds(pl.multiple_of(x * 128, 128), 128)], s_k.at[n], r_k.at[n],
                      (tm, (x + n) % 4))

    def gain_in(n):
        ox = (x - n + 4) % 4
        return remote(kslab, kfull.at[pl.ds(pl.multiple_of(ox * 128, 128), 128)], s_k.at[n], r_k.at[n], (tm, xp))

    for n in range(1, 4):
        gain_copy(n).start()
    kfull[pl.ds(pl.multiple_of(x * 128, 128), 128), :] = kslab[...]

    acc[...] = jnp.zeros_like(acc)
    own_rec.wait()
    own_meta.wait()

    def wait_record(m):
        a, b = record_copies(m)
        b.wait_recv()
        a.wait_recv()

    def gram(p, carry):
        @pl.when(p > 0)
        def _():
            wait_record(2 * p)
        wait_record(2 * p + 1)
        rows = land[p]
        marks = jnp.concatenate([mland[2 * p], mland[2 * p + 1]], axis=1)
        rows_t = rows.T
        lhs[0:512, :] = rows_t * marks[2:3, :]
        lhs[512:1024, :] = rows_t * marks[3:4, :]
        lhs[1024:1040, :] = marks
        acc[...] += jnp.dot(lhs[...], rows, preferred_element_type=F32)
        return carry

    lax.fori_loop(0, 16, gram, 0)

    for n in range(1, 4):
        gain_in(n).wait_recv()
    k_t[...] = kfull[...].T

    mine, theirs = pl.multiple_of(128 * core, 128), pl.multiple_of(128 * (1 - core), 128)

    def first_copies(d):
        return (
            remote(acc.at[pl.ds(d * 512 + theirs, 128), :], r1.at[d, :, pl.ds(0, 512)], s_1.at[2 * d], r_1.at[2 * d],
                   (sib, x)),
            remote(acc.at[pl.ds(d * 512 + 256 + theirs, 128), pl.ds(256, 256)], r1.at[d, :, pl.ds(512, 256)],
                   s_1.at[2 * d + 1], r_1.at[2 * d + 1], (sib, x)),
        )

    peers = ((sib, x), (tm, xp), (sib, xp))
    info_copies = [remote(acc.at[pl.ds(1024, 8), :], ri.at[n], s_i.at[n], r_i.at[n], peers[n]) for n in range(3)]
    for d in range(2):
        for copy in first_copies(d):
            copy.start()
    for copy in info_copies:
        copy.start()
    second = [remote(hs.at[d], r2.at[d], s_2.at[d], r_2.at[d], (tm, xp)) for d in range(2)]
    third = [remote(fh.at[d], r3.at[d], s_3.at[d], r_3.at[d], (sib, x)) for d in range(2)]
    for d in range(2):
        for copy in first_copies(d):
            copy.wait_recv()
        hs[d, :, 0:512] = acc[pl.ds(d * 512 + mine, 128), :] + r1[d, :, 0:512]
        hs[d, :, 512:768] = acc[pl.ds(d * 512 + 256 + mine, 128), 256:512] + r1[d, :, 512:768]
        second[d].start()
    for copy in info_copies:
        copy.wait_recv()
    info = (acc[1024:1032, :] + ri[0]) + (ri[1] + ri[2])

    @pl.when(jnp.logical_not(d_self))
    def _():
        d_copy.wait_recv()

    d_rows = dl[...]
    d_cols = d_rows.T

    wide[0:128, :] = prop[:, pl.ds(pl.multiple_of(j * 128, 128), 128)].T * d_rows[0:1, :]
    wide[128:136, :] = jnp.zeros((8, S), F32)
    for d in range(2):
        second[d].wait_recv()
        fh[d] = hs[d] + r2[d]
        third[d].start()
        om[d, pl.ds(mine, 128), :] = fh[d, :, 0:512]
        om[d, pl.ds(256 + mine, 128), 256:512] = fh[d, :, 512:768]
        third[d].wait_recv()
        om[d, pl.ds(theirs, 128), :] = r3[d, :, 0:512]
        om[d, pl.ds(256 + theirs, 128), 256:512] = r3[d, :, 512:768]
        om[d, 256:512, 0:256] = om[d, 0:256, 256:512].T
        if d == 1:
            wide[...] = dot_nt(wide[...], prop[...]) * d_rows[1:2, :]
        w = wide[...]
        seen = jnp.concatenate([jnp.zeros((128, S), F32), jnp.broadcast_to(info[d:d + 1, :], (8, S))], axis=0)
        wide[...] = w - dot(dot(w, om[d]) - seen, cov[...])

    lead = (lead_tm, 1)
    slab_cols = pl.multiple_of(j * 128, 128)
    even_copy = remote(slab_t, maps.at[e_me, :, pl.ds(slab_cols, 128)], s_a.at[0], r_a.at[e_me * 4 + j], lead)
    odd_copy = remote(slab, maps.at[e_me, pl.ds(slab_cols, 128), :], s_a.at[0], r_a.at[e_me * 4 + j], lead)
    b_copy = remote(brow, brows.at[e_me], s_b.at[0], r_b.at[e_me], lead)

    @pl.when(q == 0)
    def _():
        slab_t[...] = wide[0:128, :].T

    @pl.when(q == 1)
    def _():
        slab[...] = wide[0:128, :]

    @pl.when(is_lead)
    def _():
        maps[0, :, 256:384] = slab_t[...]

    even_send = jnp.logical_and(q == 0, jnp.logical_not(is_lead))

    @pl.when(even_send)
    def _():
        even_copy.start()

    @pl.when(q == 1)
    def _():
        odd_copy.start()

    brow[...] = wide[128:136, :]

    @pl.when(j == 0)
    def _():
        b_copy.start()

    next_g = (g + 1) % 4
    hop_copy = remote(hop_src, hop_in, s_h.at[0], r_h.at[0], (next_g * 8 + (2 * (next_g % 2)) * 2, 1))

    def start_copy(e, n):
        sy, sz = row_place(4 * g + e // 2)
        return remote(start_src.at[e], start_in, s_s.at[e * 4 + n], r_s.at[0],
                      (sz * 8 + sy * 2 + n % 2, 2 * (e % 2) + n // 2))

    @pl.when(is_lead)
    def _():
        @pl.when(g == 0)
        def _():
            for ox in (0, 2, 3):
                remote(psrc, pr.at[ox], s_p.at[0], r_p.at[ox], (0, 0)).wait_recv()
            for ox in range(4):
                hop_in[:, 128 * ox:128 * ox + 128] = pr[ox]

        for e in range(8):
            for n in range(4):
                if (e, n) == (0, 2):
                    continue
                if e % 2 == 0:
                    remote(slab_t, maps.at[e, :, pl.ds(128 * n, 128)], s_a.at[0], r_a.at[e * 4 + n],
                           (sib, x)).wait_recv()
                else:
                    remote(slab, maps.at[e, pl.ds(128 * n, 128), :], s_a.at[0], r_a.at[e * 4 + n],
                           (sib, x)).wait_recv()
            remote(brow, brows.at[e], s_b.at[0], r_b.at[e], (sib, x)).wait_recv()

        @pl.when(g > 0)
        def _():
            hop_copy.wait_recv()

        row = hop_in[0:1, :]
        for e in range(0, 8, 2):
            start_src[e] = jnp.broadcast_to(row, (8, S))
            for n in range(4):
                if (e, n) != (0, 2):
                    start_copy(e, n).start()
            if e == 0:
                start_in[...] = start_src[0]
            col = row_times(maps.at[e], row) + brows[e].T[:, 0:1]
            row = col_times(maps.at[e + 1], col) + brows[e + 1, 0:1, :]
            if e == 6:
                hop_src[...] = jnp.broadcast_to(row, (8, S))

                @pl.when(g < 3)
                def _():
                    hop_copy.start()
            start_src[e + 1] = jnp.broadcast_to(to_row(col), (8, S))
            for n in range(4):
                start_copy(e + 1, n).start()

    @pl.when(jnp.logical_not(is_lead))
    def _():
        start_copy(0, 0).wait_recv()

    before = start_in[0:1, :]
    moved = d_cols[:, 0:1] * row_times(prop, before)
    first_col = moved - row_times(cov, col_times(om.at[0], moved) - info[0:1, :])
    first = to_row(first_col)
    ahead_col = row_times(prop, first)
    moved = d_cols[:, 1:2] * ahead_col
    second_col = moved - row_times(cov, col_times(om.at[1], moved) - info[1:2, :])
    last = to_row(second_col)
    msg[0:1, :] = first
    msg[1:2, :] = last
    msg[2:3, :] = to_row(ahead_col)
    msg[3:4, :] = to_row(row_times(prop, last))
    msg[4:6, :] = d_rows[0:2, :]
    msg[6:8, :] = jnp.zeros((2, S), F32)

    def mail_copy(n):
        return remote(msg, mail.at[c_me], s_m.at[n], r_m.at[c_me], ((tm + n) % 32, j))

    to_self = j == x

    @pl.when(to_self)
    def _():
        mail[c_me] = msg[...]

    @pl.when(jnp.logical_not(to_self))
    def _():
        mail_copy(0).start()

    def post(n, carry):
        mail_copy(n).start()
        return carry

    lax.fori_loop(1, 32, post, 0)

    def wait_mail(c):
        @pl.when(jnp.logical_not(jnp.logical_and(to_self, c == c_me)))
        def _():
            remote(msg, mail.at[c], s_m.at[0], r_m.at[c], (sib, x)).wait_recv()

    own_cols = pl.ds(pl.multiple_of(x * 128, 128), 128)

    def back(n, carry):
        state, damp_next = carry
        c = 31 - n
        wait_mail(c)
        rows = mail[c]
        cols = rows.T
        gap = damp_next * (state - damp_next * rows[3:4, :])
        later = cols[:, 1:2] + row_times(kfull, gap)
        gap_col = cols[:, 5:6] * (later - cols[:, 5:6] * cols[:, 2:3])
        state = rows[0:1, :] + col_times(k_t, gap_col)

        @pl.when(c == tm)
        def _():
            hs[0, 0:1, 0:512] = state
            hs[0, 8:9, 0:512] = to_row(later)

        return state, rows[4:5, :]

    for d in range(2):
        second[d].wait_send()
    zero = jnp.zeros((1, S), F32)
    lax.fori_loop(0, 32 - tm, back, (zero, zero))
    smooth_out[0:1, :] = hs[0, 0:1, own_cols]
    smooth_out[1:2, :] = hs[0, 8:9, own_cols]
    filt_out[...] = mail[tm, 0:2, own_cols]

    def drain_mail(n, carry):
        wait_mail(n)
        return carry

    lax.fori_loop(0, tm, drain_mail, 0)

    def drain_record(m, carry):
        a, b = record_copies(m)
        a.wait_send()
        b.wait_send()
        return carry

    lax.fori_loop(1, 32, drain_record, 0)

    def drain_post(n, carry):
        mail_copy(n).wait_send()
        return carry

    lax.fori_loop(1, 32, drain_post, 0)

    @pl.when(jnp.logical_not(to_self))
    def _():
        mail_copy(0).wait_send()

    for n in range(1, 4):
        gain_copy(n).wait_send()

    @pl.when(jnp.logical_not(d_self))
    def _():
        d_copy.wait_send()

    @pl.when(p_send)
    def _():
        p_copy.wait_send()

    for d in range(2):
        for copy in first_copies(d):
            copy.wait_send()
        third[d].wait_send()
    for copy in info_copies:
        copy.wait_send()

    @pl.when(even_send)
    def _():
        even_copy.wait_send()

    @pl.when(q == 1)
    def _():
        odd_copy.wait_send()

    @pl.when(j == 0)
    def _():
        b_copy.wait_send()

    @pl.when(is_lead)
    def _():
        for e in range(8):
            for n in range(4):
                if (e, n) != (0, 2):
                    start_copy(e, n).wait_send()

        @pl.when(g < 3)
        def _():
            hop_copy.wait_send()


def local(records, obs_values, block_day, block_count, propagator_matrix, analysis_cov, unattenuated_multiplier,
          damping, prior_mean):
    slot = lax.broadcasted_iota(jnp.int32, (32, 16, 128), 2)
    part = lax.broadcasted_iota(jnp.int32, (32, 16, 128), 1)
    held = jnp.logical_and(slot < block_count[:, None, None], block_day[:, None, None] == part % 2)
    held = jnp.logical_and(held, part < 4)
    values = jnp.where(part < 2, obs_values.reshape(32, 1, 128), jnp.ones((), BF16))
    meta = jnp.where(held, values, jnp.zeros((), BF16))
    vmem = pl.BlockSpec(memory_space=pltpu.VMEM)
    dma = pltpu.SemaphoreType.DMA
    return pl.pallas_call(
        kernel,
        out_shape=(jax.ShapeDtypeStruct((2, 128), F32), jax.ShapeDtypeStruct((2, 128), F32)),
        in_specs=[pl.BlockSpec(memory_space=pl.ANY)] + [vmem] * 6,
        out_specs=(vmem, vmem),
        scratch_shapes=[
            pltpu.VMEM((16, 256, S), BF16),
            pltpu.VMEM((32, 16, 128), BF16),
            pltpu.VMEM((1040, 256), BF16),
            pltpu.VMEM((1040, S), F32),
            pltpu.VMEM((2, 128, 768), F32),
            pltpu.VMEM((2, 128, 768), F32),
            pltpu.VMEM((2, 128, 768), F32),
            pltpu.VMEM((2, 128, 768), F32),
            pltpu.VMEM((2, 128, 768), F32),
            pltpu.VMEM((3, 8, S), F32),
            pltpu.VMEM((2, S, S), F32),
            pltpu.VMEM((136, S), F32),
            pltpu.VMEM((128, S), F32),
            pltpu.VMEM((S, 128), F32),
            pltpu.VMEM((8, S), F32),
            pltpu.VMEM((8, S, S), F32),
            pltpu.VMEM((8, 8, S), F32),
            pltpu.VMEM((S, S), F32),
            pltpu.VMEM((S, S), F32),
            pltpu.VMEM((8, S), F32),
            pltpu.VMEM((8, S), F32),
            pltpu.VMEM((8, 128), F32),
            pltpu.VMEM((4, 8, 128), F32),
            pltpu.VMEM((8, S), F32),
            pltpu.VMEM((8, S), F32),
            pltpu.VMEM((8, 8, S), F32),
            pltpu.VMEM((8, S), F32),
            pltpu.VMEM((8, S), F32),
            pltpu.VMEM((32, 8, S), F32),
            dma((32,)), dma((32,)), dma((32,)), dma((32,)),
            dma((4,)), dma((4,)), dma((1,)), dma((1,)), dma((1,)), dma((4,)),
            dma((4,)), dma((4,)), dma((3,)), dma((3,)), dma((2,)), dma((2,)), dma((2,)), dma((2,)),
            dma((1,)), dma((32,)), dma((1,)), dma((8,)), dma((1,)), dma((1,)),
            dma((32,)), dma((1,)), dma((32,)), dma((32,)), dma, dma,
        ],
        compiler_params=pltpu.CompilerParams(collective_id=0, has_side_effects=True, vmem_limit_bytes=56 << 20),
        cost_estimate=pl.CostEstimate(flops=10**10, bytes_accessed=10**8, transcendentals=0),
    )(records, meta, propagator_matrix, analysis_cov, unattenuated_multiplier, damping, prior_mean.reshape(1, 128))


def solution(mesh):
    return jax.shard_map(
        local,
        mesh=mesh,
        in_specs=(
            P(("tm", "obs"), None),
            P(("tm", "obs")),
            P(("tm", "obs")),
            P(("tm", "obs")),
            P(),
            P(),
            P("obs", None),
            P("tm", None),
            P("obs"),
        ),
        out_specs=(P("tm", "obs"), P("tm", "obs")),
        check_vma=False,
    )
```

```python
import jax
import jax.numpy as jnp
from jax import lax
from jax.experimental import pallas as pl
from jax.experimental.pallas import tpu as pltpu
from jax.sharding import PartitionSpec as P

MESH = pl.DeviceIdType.MESH
F32 = jnp.float32
BF16 = jnp.bfloat16
HIGH = lax.Precision.HIGHEST
S = 512


def row_place(r):
    g, i = r // 4, r % 4
    im = i % 3
    return (2 * (g % 2) + im * (im + 1) // 2) % 4, (g + i // 3) % 4


def place_row(y, z):
    phi = (y + 2 * z) % 4
    i = phi + (phi // 2) * (5 - 2 * phi)
    g = (z - i // 3 + 4) % 4
    return g, i


def row_times(ref, row):
    wide = jnp.broadcast_to(row, (8, S))
    tiles = []
    for k in range(0, S, 8):
        t = [ref[k:k + 8, n:n + 128] * wide[:, n:n + 128] for n in range(0, S, 128)]
        tiles.append(jnp.broadcast_to(jnp.sum((t[0] + t[1]) + (t[2] + t[3]), axis=1, keepdims=True), (8, 128)))
    return tiles


def col_times(ref, tiles):
    out = []
    for n in range(0, S, 128):
        total = [None] * 4
        for k in range(64):
            p = ref[8 * k:8 * k + 8, n:n + 128] * tiles[k]
            total[k % 4] = p if total[k % 4] is None else total[k % 4] + p
        out.append(jnp.sum((total[0] + total[1]) + (total[2] + total[3]), axis=0, keepdims=True))
    return jnp.concatenate(out, axis=1)


def diagonals():
    lead = lax.broadcasted_iota(jnp.int32, (8, 128), 1) - lax.broadcasted_iota(jnp.int32, (8, 128), 0)
    return [lead == 8 * k for k in range(16)]


def to_row(tiles):
    marks = diagonals()
    out = []
    for n in range(4):
        picked = [jnp.where(marks[k], tiles[16 * n + k], 0.0) for k in range(16)]
        while len(picked) > 1:
            picked = [picked[k] + picked[k + 1] for k in range(0, len(picked), 2)]
        out.append(jnp.sum(picked[0], axis=0, keepdims=True))
    return jnp.concatenate(out, axis=1)


def to_tiles(row):
    marks = diagonals()
    tiles = []
    for n in range(4):
        part = jnp.broadcast_to(row[:, 128 * n:128 * n + 128], (8, 128))
        for k in range(16):
            tiles.append(jnp.broadcast_to(
                jnp.sum(jnp.where(marks[k], part, 0.0), axis=1, keepdims=True), (8, 128)))
    return tiles


def keep(ref, tiles):
    for k in range(64):
        ref[8 * k:8 * k + 8, :] = tiles[k]


def kept_tile(ref, k):
    return ref[8 * k:8 * k + 8, :]


def dot(a, b):
    return jnp.dot(a, b, precision=HIGH, preferred_element_type=F32)


def dot_nt(a, b):
    return lax.dot_general(a, b, (((1,), (1,)), ((), ())), precision=HIGH, preferred_element_type=F32)


def kernel(rec, meta, prop, cov, kslab, damp, prior, filt_out, smooth_out,
           land, mland, lhs, acc, r1, hs, r2, fh, r3, ri, om, wide, slab, slab_t, brow, maps, brows, kfull, k_t,
           dsrc, dl, psrc, pr, hop_src, hop_in, start_src, start_in, msg, mail, kept, mail_tiles, d_tiles, b_tiles,
           s_rec, r_rec, s_meta, r_meta, s_k, r_k, s_d, r_d, s_p, r_p, s_1, r_1, s_i, r_i, s_2, r_2, s_3, r_3,
           s_a, r_a, s_b, r_b, s_h, r_h, s_s, r_s, s_m, r_m, l_rec, l_meta):
    tm, x = lax.axis_index("tm"), lax.axis_index("obs")
    z, y, core = tm // 8, (tm // 2) % 4, tm % 2
    q, xi = x // 2, x % 2
    g, i_row = place_row(y, z)
    e_me = 2 * i_row + q
    c_me = 8 * g + e_me
    j = 2 * xi + core
    lead_tm = g * 8 + (2 * (g % 2)) * 2
    is_lead = jnp.logical_and(tm == lead_tm, x == 1)
    sib = tm + 1 - 2 * core
    xp = x + 1 - 2 * xi

    def remote(src, dst, ss, rs, dev):
        return pltpu.make_async_remote_copy(src_ref=src, dst_ref=dst, send_sem=ss, recv_sem=rs, device_id=dev,
                                            device_id_type=MESH)

    drains = []

    def sent(copy, when=None):
        if when is None:
            drains.append(copy.wait_send)
        else:
            drains.append(lambda: pl.when(when)(copy.wait_send))

    barrier = pltpu.get_barrier_semaphore()

    def owner_of(o):
        dq, dy, dz = o // 16, (o // 4) % 4, o % 4
        return ((z + dz) % 4, (y + dy) % 4, (q + dq) % 2, x + dq * (3 - 2 * x)), (
            ((z - dz + 4) % 4) * 8 + ((y - dy + 4) % 4) * 2 + core, x + dq * (3 - 2 * x))

    dr_y, dr_z = row_place(tm // 2)
    d_tm, d_x = dr_z * 8 + dr_y * 2 + x % 2, 2 * (tm % 2) + x // 2
    d_self = jnp.logical_and(d_tm == tm, d_x == x)

    def greet(dev):
        pl.semaphore_signal(barrier, 1, device_id=dev, device_id_type=MESH)

    def greet_source(o, carry):
        greet(owner_of(o)[1])
        return carry

    lax.fori_loop(1, 32, greet_source, 0)
    for dev in ((tm, (x + 1) % 4), (tm, (x + 2) % 4), (tm, (x + 3) % 4), (sib, x), (sib, xp),
                (c_me, 2 * xi + core)):
        greet(dev)
    pl.semaphore_wait(barrier, 37)

    def offset(m):
        return 1 + ((m - 1) * 11 + core * 15) % 31

    def record_copies(m):
        o = offset(m)
        tz, ty, tq, tx = owner_of(o)[0]
        tg, ti = place_row(ty, tz)
        c = 8 * tg + 2 * ti + tq
        dev = (tz * 8 + ty * 2 + core, tx)
        return (
            remote(rec.at[pl.ds(pl.multiple_of(c * 128, 128), 128)],
                   land.at[m // 2, pl.ds(pl.multiple_of((m % 2) * 128, 128), 128)], s_rec.at[m], r_rec.at[m], dev),
            remote(meta.at[c], mland.at[m], s_meta.at[m], r_meta.at[m], dev),
        )

    own_rec = pltpu.make_async_copy(rec.at[pl.ds(pl.multiple_of(c_me * 128, 128), 128)],
                                    land.at[0, pl.ds(0, 128)], l_rec)
    own_rec.start()
    own_meta = pltpu.make_async_copy(meta.at[c_me], mland.at[0], l_meta)
    own_meta.start()

    def send_record(m, carry):
        a, b = record_copies(m)
        b.start()
        a.start()
        return carry

    dsrc[...] = jnp.zeros_like(dsrc)
    dsrc[0:2, :] = damp[...]
    d_copy = remote(dsrc, dl, s_d.at[0], r_d.at[0], (d_tm, d_x))

    @pl.when(d_self)
    def _():
        dl[...] = dsrc[...]

    @pl.when(jnp.logical_not(d_self))
    def _():
        d_copy.start()

    sent(d_copy, jnp.logical_not(d_self))

    psrc[...] = jnp.broadcast_to(prior[...], (8, 128))
    p_copy = remote(psrc, pr.at[x], s_p.at[0], r_p.at[x], (0, 1))
    p_send = jnp.logical_and(tm == 0, x != 1)

    @pl.when(p_send)
    def _():
        p_copy.start()

    sent(p_copy, p_send)

    @pl.when(jnp.logical_and(tm == 0, x == 1))
    def _():
        pr[1] = psrc[...]

    lax.fori_loop(1, 32, send_record, 0)

    def drain_record(m, carry):
        a, b = record_copies(m)
        a.wait_send()
        b.wait_send()
        return carry

    drains.append(lambda: lax.fori_loop(1, 32, drain_record, 0))

    def gain_copy(n):
        return remote(kslab, kfull.at[pl.ds(pl.multiple_of(x * 128, 128), 128)], s_k.at[n], r_k.at[n],
                      (tm, (x + n) % 4))

    def gain_in(n):
        ox = (x - n + 4) % 4
        return remote(kslab, kfull.at[pl.ds(pl.multiple_of(ox * 128, 128), 128)], s_k.at[n], r_k.at[n], (tm, xp))

    for n in range(1, 4):
        gain_copy(n).start()
        sent(gain_copy(n))
    kfull[pl.ds(pl.multiple_of(x * 128, 128), 128), :] = kslab[...]

    acc[...] = jnp.zeros_like(acc)
    own_rec.wait()
    own_meta.wait()

    def wait_record(m):
        a, b = record_copies(m)
        b.wait_recv()
        a.wait_recv()

    def gram(p, carry):
        @pl.when(p > 0)
        def _():
            wait_record(2 * p)
        wait_record(2 * p + 1)
        rows = land[p]
        marks = jnp.concatenate([mland[2 * p], mland[2 * p + 1]], axis=1)
        rows_t = rows.T
        lhs[0:512, :] = rows_t * marks[2:3, :]
        lhs[512:1024, :] = rows_t * marks[3:4, :]
        lhs[1024:1040, :] = marks
        acc[...] += jnp.dot(lhs[...], rows, preferred_element_type=F32)
        return carry

    lax.fori_loop(0, 16, gram, 0)

    for n in range(1, 4):
        gain_in(n).wait_recv()
    k_t[...] = kfull[...].T

    mine, theirs = pl.multiple_of(128 * core, 128), pl.multiple_of(128 * (1 - core), 128)

    def first_copies(d):
        return (
            remote(acc.at[pl.ds(d * 512 + theirs, 128), :], r1.at[d, :, pl.ds(0, 512)], s_1.at[2 * d], r_1.at[2 * d],
                   (sib, x)),
            remote(acc.at[pl.ds(d * 512 + 256 + theirs, 128), pl.ds(256, 256)], r1.at[d, :, pl.ds(512, 256)],
                   s_1.at[2 * d + 1], r_1.at[2 * d + 1], (sib, x)),
        )

    peers = ((sib, x), (tm, xp), (sib, xp))
    info_copies = [remote(acc.at[pl.ds(1024, 8), :], ri.at[n], s_i.at[n], r_i.at[n], peers[n]) for n in range(3)]
    for d in range(2):
        for copy in first_copies(d):
            copy.start()
            sent(copy)
    for copy in info_copies:
        copy.start()
        sent(copy)
    second = [remote(hs.at[d], r2.at[d], s_2.at[d], r_2.at[d], (tm, xp)) for d in range(2)]
    third = [remote(fh.at[d], r3.at[d], s_3.at[d], r_3.at[d], (sib, x)) for d in range(2)]
    for d in range(2):
        for copy in first_copies(d):
            copy.wait_recv()
        hs[d, :, 0:512] = acc[pl.ds(d * 512 + mine, 128), :] + r1[d, :, 0:512]
        hs[d, :, 512:768] = acc[pl.ds(d * 512 + 256 + mine, 128), 256:512] + r1[d, :, 512:768]
        second[d].start()
        sent(second[d])
    for copy in info_copies:
        copy.wait_recv()
    info = (acc[1024:1032, :] + ri[0]) + (ri[1] + ri[2])

    @pl.when(jnp.logical_not(d_self))
    def _():
        d_copy.wait_recv()

    d_rows = dl[...]
    for d in range(2):
        keep(d_tiles.at[d], to_tiles(d_rows[d:d + 1, :]))

    wide[0:128, :] = prop[:, pl.ds(pl.multiple_of(j * 128, 128), 128)].T * d_rows[0:1, :]
    wide[128:136, :] = jnp.zeros((8, S), F32)
    for d in range(2):
        second[d].wait_recv()
        fh[d] = hs[d] + r2[d]
        third[d].start()
        sent(third[d])
        om[d, pl.ds(mine, 128), :] = fh[d, :, 0:512]
        om[d, pl.ds(256 + mine, 128), 256:512] = fh[d, :, 512:768]
        third[d].wait_recv()
        om[d, pl.ds(theirs, 128), :] = r3[d, :, 0:512]
        om[d, pl.ds(256 + theirs, 128), 256:512] = r3[d, :, 512:768]
        om[d, 256:512, 0:256] = om[d, 0:256, 256:512].T
        if d == 1:
            wide[...] = dot_nt(wide[...], prop[...]) * d_rows[1:2, :]
        w = wide[...]
        seen = jnp.concatenate([jnp.zeros((128, S), F32), jnp.broadcast_to(info[d:d + 1, :], (8, S))], axis=0)
        wide[...] = w - dot(dot(w, om[d]) - seen, cov[...])

    lead = (lead_tm, 1)
    slab_cols = pl.multiple_of(j * 128, 128)
    even_copy = remote(slab_t, maps.at[e_me, :, pl.ds(slab_cols, 128)], s_a.at[0], r_a.at[e_me * 4 + j], lead)
    odd_copy = remote(slab, maps.at[e_me, pl.ds(slab_cols, 128), :], s_a.at[0], r_a.at[e_me * 4 + j], lead)
    b_copy = remote(brow, brows.at[e_me], s_b.at[0], r_b.at[e_me], lead)

    @pl.when(q == 0)
    def _():
        slab_t[...] = wide[0:128, :].T

    @pl.when(q == 1)
    def _():
        slab[...] = wide[0:128, :]

    @pl.when(is_lead)
    def _():
        maps[0, :, 256:384] = slab_t[...]

    even_send = jnp.logical_and(q == 0, jnp.logical_not(is_lead))

    @pl.when(even_send)
    def _():
        even_copy.start()

    sent(even_copy, even_send)

    @pl.when(q == 1)
    def _():
        odd_copy.start()

    sent(odd_copy, q == 1)

    brow[...] = wide[128:136, :]

    @pl.when(j == 0)
    def _():
        b_copy.start()

    sent(b_copy, j == 0)

    next_g = (g + 1) % 4
    hop_copy = remote(hop_src, hop_in, s_h.at[0], r_h.at[0], (next_g * 8 + (2 * (next_g % 2)) * 2, 1))

    def start_copy(e, n):
        sy, sz = row_place(4 * g + e // 2)
        return remote(start_src.at[e], start_in, s_s.at[e * 4 + n], r_s.at[0],
                      (sz * 8 + sy * 2 + n % 2, 2 * (e % 2) + n // 2))

    @pl.when(is_lead)
    def _():
        @pl.when(g == 0)
        def _():
            for ox in (0, 2, 3):
                remote(psrc, pr.at[ox], s_p.at[0], r_p.at[ox], (0, 0)).wait_recv()
            for ox in range(4):
                hop_in[:, 128 * ox:128 * ox + 128] = pr[ox]

        for e in range(8):
            for n in range(4):
                if (e, n) == (0, 2):
                    continue
                if e % 2 == 0:
                    remote(slab_t, maps.at[e, :, pl.ds(128 * n, 128)], s_a.at[0], r_a.at[e * 4 + n],
                           (sib, x)).wait_recv()
                else:
                    remote(slab, maps.at[e, pl.ds(128 * n, 128), :], s_a.at[0], r_a.at[e * 4 + n],
                           (sib, x)).wait_recv()
            remote(brow, brows.at[e], s_b.at[0], r_b.at[e], (sib, x)).wait_recv()

        for e in range(0, 8, 2):
            keep(b_tiles.at[e // 2], to_tiles(brows[e, 0:1, :]))

        @pl.when(g > 0)
        def _():
            hop_copy.wait_recv()

        row = hop_in[0:1, :]
        for e in range(0, 8, 2):
            start_src[e] = jnp.broadcast_to(row, (8, S))
            tiles = row_times(maps.at[e], row)
            tiles = [tiles[k] + kept_tile(b_tiles.at[e // 2], k) for k in range(64)]
            row = col_times(maps.at[e + 1], tiles) + brows[e + 1, 0:1, :]
            start_src[e + 1] = jnp.broadcast_to(to_row(tiles), (8, S))
        hop_src[...] = jnp.broadcast_to(row, (8, S))

        @pl.when(g < 3)
        def _():
            hop_copy.start()

        start_in[...] = start_src[0]
        for e in range(7, -1, -1):
            for n in range(4):
                if (e, n) != (0, 2):
                    start_copy(e, n).start()

    def drain_leader():
        for e in range(8):
            for n in range(4):
                if (e, n) != (0, 2):
                    start_copy(e, n).wait_send()

        @pl.when(g < 3)
        def _():
            hop_copy.wait_send()

    drains.append(lambda: pl.when(is_lead)(drain_leader))

    @pl.when(jnp.logical_not(is_lead))
    def _():
        start_copy(0, 0).wait_recv()

    before = start_in[0:1, :]

    def day(d, ahead):
        moved = [kept_tile(d_tiles.at[d], k) * ahead[k] for k in range(64)]
        back = row_times(cov, col_times(om.at[d], moved) - info[d:d + 1, :])
        return to_row([moved[k] - back[k] for k in range(64)])

    first = day(0, row_times(prop, before))
    ahead = row_times(prop, first)
    last = day(1, ahead)
    d_first, d_last = d_rows[0:1, :], d_rows[1:2, :]
    msg[0:1, :] = first
    msg[1:2, :] = last
    msg[2:3, :] = d_last * (last - d_last * to_row(ahead))
    msg[3:4, :] = to_row(row_times(prop, last))
    msg[4:5, :] = d_first
    msg[5:6, :] = d_last
    msg[6:8, :] = jnp.zeros((2, S), F32)

    def mail_copy(n):
        return remote(msg, mail.at[c_me], s_m.at[n], r_m.at[c_me], (n, j))

    to_self = j == x

    @pl.when(to_self)
    def _():
        mail[c_me] = msg[...]

    def to_other(n):
        return jnp.logical_or(n != tm, jnp.logical_not(to_self))

    def post(n, carry):
        @pl.when(to_other(n))
        def _():
            mail_copy(n).start()
        return carry

    lax.fori_loop(0, 32, post, 0)

    def drain_post(n, carry):
        @pl.when(to_other(n))
        def _():
            mail_copy(n).wait_send()
        return carry

    drains.append(lambda: lax.fori_loop(0, 32, drain_post, 0))

    def wait_mail(c):
        @pl.when(jnp.logical_not(jnp.logical_and(to_self, c == c_me)))
        def _():
            remote(msg, mail.at[c], s_m.at[0], r_m.at[c], (sib, x)).wait_recv()

    own_cols = pl.ds(pl.multiple_of(x * 128, 128), 128)

    def expand(c, carry):
        wait_mail(c)
        keep(mail_tiles.at[c, 0], to_tiles(mail[c, 5:6, :]))
        keep(mail_tiles.at[c, 1], to_tiles(mail[c, 2:3, :]))
        return carry

    lax.fori_loop(tm, 32, expand, 0)

    def back(c, state, damp_next):
        gap = damp_next * (state - damp_next * mail[c, 3:4, :])
        later = row_times(kfull, gap)
        scale, shift = mail_tiles.at[c, 0], mail_tiles.at[c, 1]
        gaps = [kept_tile(scale, k) * later[k] + kept_tile(shift, k) for k in range(64)]
        return mail[c, 0:1, :] + col_times(k_t, gaps), later

    def back_step(n, carry):
        state, damp_next = carry
        c = 31 - n
        return back(c, state, damp_next)[0], mail[c, 4:5, :]

    zero = jnp.zeros((1, S), F32)
    state, damp_next = lax.fori_loop(0, 31 - tm, back_step, (zero, zero))
    state, later = back(tm, state, damp_next)
    kept[0:1, :] = state
    kept[1:2, :] = mail[tm, 1:2, :] + to_row(later)
    smooth_out[...] = kept[0:2, own_cols]
    filt_out[...] = mail[tm, 0:2, own_cols]

    def drain_mail(n, carry):
        wait_mail(n)
        return carry

    lax.fori_loop(0, tm, drain_mail, 0)
    for drain in drains:
        drain()


def local(records, obs_values, block_day, block_count, propagator_matrix, analysis_cov, unattenuated_multiplier,
          damping, prior_mean):
    slot = lax.broadcasted_iota(jnp.int32, (32, 16, 128), 2)
    part = lax.broadcasted_iota(jnp.int32, (32, 16, 128), 1)
    held = jnp.logical_and(slot < block_count[:, None, None], block_day[:, None, None] == part % 2)
    held = jnp.logical_and(held, part < 4)
    values = jnp.where(part < 2, obs_values.reshape(32, 1, 128), jnp.ones((), BF16))
    meta = jnp.where(held, values, jnp.zeros((), BF16))
    vmem = pl.BlockSpec(memory_space=pltpu.VMEM)
    dma = pltpu.SemaphoreType.DMA
    return pl.pallas_call(
        kernel,
        out_shape=(jax.ShapeDtypeStruct((2, 128), F32), jax.ShapeDtypeStruct((2, 128), F32)),
        in_specs=[pl.BlockSpec(memory_space=pl.ANY)] + [vmem] * 6,
        out_specs=(vmem, vmem),
        scratch_shapes=[
            pltpu.VMEM((16, 256, S), BF16),
            pltpu.VMEM((32, 16, 128), BF16),
            pltpu.VMEM((1040, 256), BF16),
            pltpu.VMEM((1040, S), F32),
            pltpu.VMEM((2, 128, 768), F32),
            pltpu.VMEM((2, 128, 768), F32),
            pltpu.VMEM((2, 128, 768), F32),
            pltpu.VMEM((2, 128, 768), F32),
            pltpu.VMEM((2, 128, 768), F32),
            pltpu.VMEM((3, 8, S), F32),
            pltpu.VMEM((2, S, S), F32),
            pltpu.VMEM((136, S), F32),
            pltpu.VMEM((128, S), F32),
            pltpu.VMEM((S, 128), F32),
            pltpu.VMEM((8, S), F32),
            pltpu.VMEM((8, S, S), F32),
            pltpu.VMEM((8, 8, S), F32),
            pltpu.VMEM((S, S), F32),
            pltpu.VMEM((S, S), F32),
            pltpu.VMEM((8, S), F32),
            pltpu.VMEM((8, S), F32),
            pltpu.VMEM((8, 128), F32),
            pltpu.VMEM((4, 8, 128), F32),
            pltpu.VMEM((8, S), F32),
            pltpu.VMEM((8, S), F32),
            pltpu.VMEM((8, 8, S), F32),
            pltpu.VMEM((8, S), F32),
            pltpu.VMEM((8, S), F32),
            pltpu.VMEM((32, 8, S), F32),
            pltpu.VMEM((8, S), F32),
            pltpu.VMEM((32, 2, S, 128), F32),
            pltpu.VMEM((2, S, 128), F32),
            pltpu.VMEM((4, S, 128), F32),
            dma((32,)), dma((32,)), dma((32,)), dma((32,)),
            dma((4,)), dma((4,)), dma((1,)), dma((1,)), dma((1,)), dma((4,)),
            dma((4,)), dma((4,)), dma((3,)), dma((3,)), dma((2,)), dma((2,)), dma((2,)), dma((2,)),
            dma((1,)), dma((32,)), dma((1,)), dma((8,)), dma((1,)), dma((1,)),
            dma((32,)), dma((1,)), dma((32,)), dma((32,)), dma, dma,
        ],
        compiler_params=pltpu.CompilerParams(collective_id=0, has_side_effects=True, vmem_limit_bytes=56 << 20),
        cost_estimate=pl.CostEstimate(flops=10**10, bytes_accessed=10**8, transcendentals=0),
    )(records, meta, propagator_matrix, analysis_cov, unattenuated_multiplier, damping, prior_mean.reshape(1, 128))


def solution(mesh):
    return jax.shard_map(
        local,
        mesh=mesh,
        in_specs=(
            P(("tm", "obs"), None),
            P(("tm", "obs")),
            P(("tm", "obs")),
            P(("tm", "obs")),
            P(),
            P(),
            P("obs", None),
            P("tm", None),
            P("obs"),
        ),
        out_specs=(P("tm", "obs"), P("tm", "obs")),
        check_vma=False,
    )
```

```python
import jax
import jax.numpy as jnp
from jax import lax
from jax.experimental import pallas as pl
from jax.experimental.pallas import tpu as pltpu
from jax.sharding import PartitionSpec as P

MESH = pl.DeviceIdType.MESH
F32 = jnp.float32
BF16 = jnp.bfloat16
HIGH = lax.Precision.HIGHEST
S = 512


def row_place(r):
    g, i = 3 - r // 4, r % 4
    im = i % 3
    return (2 * (g // 2) + im * (im + 1) // 2) % 4, g + (i // 3) * (3 - 2 * g)


def place_row(y, z):
    odd = y % 2
    extra = (1 - odd) * ((y // 2 + z // 2) % 2)
    g = z + extra * (3 - 2 * z)
    return 3 - g, odd * (1 + ((y - 2 * (z // 2) + 4) % 4) // 2) + 3 * extra


def lead_of(g):
    return (3 - g) * 8 + (3 - g) // 2 * 4


PARTS = (((0, 0, 512, 0), (3, 384, 128, 512)), ((1, 128, 384, 0), (2, 256, 256, 384)))


def row_times(ref, row):
    wide = jnp.broadcast_to(row, (8, S))
    tiles = []
    for k in range(0, S, 8):
        t = [ref[k:k + 8, n:n + 128] * wide[:, n:n + 128] for n in range(0, S, 128)]
        tiles.append(jnp.broadcast_to(jnp.sum((t[0] + t[1]) + (t[2] + t[3]), axis=1, keepdims=True), (8, 128)))
    return tiles


def col_times(ref, tiles):
    out = []
    for n in range(0, S, 128):
        total = [None] * 4
        for k in range(64):
            p = ref[8 * k:8 * k + 8, n:n + 128] * tiles[k]
            total[k % 4] = p if total[k % 4] is None else total[k % 4] + p
        out.append(jnp.sum((total[0] + total[1]) + (total[2] + total[3]), axis=0, keepdims=True))
    return jnp.concatenate(out, axis=1)


def diagonals():
    lead = lax.broadcasted_iota(jnp.int32, (8, 128), 1) - lax.broadcasted_iota(jnp.int32, (8, 128), 0)
    return [lead == 8 * k for k in range(16)]


def to_row(tiles):
    marks = diagonals()
    out = []
    for n in range(4):
        picked = [jnp.where(marks[k], tiles[16 * n + k], 0.0) for k in range(16)]
        while len(picked) > 1:
            picked = [picked[k] + picked[k + 1] for k in range(0, len(picked), 2)]
        out.append(jnp.sum(picked[0], axis=0, keepdims=True))
    return jnp.concatenate(out, axis=1)


def to_tiles(row):
    marks = diagonals()
    tiles = []
    for n in range(4):
        part = jnp.broadcast_to(row[:, 128 * n:128 * n + 128], (8, 128))
        for k in range(16):
            tiles.append(jnp.broadcast_to(
                jnp.sum(jnp.where(marks[k], part, 0.0), axis=1, keepdims=True), (8, 128)))
    return tiles


def keep(ref, tiles):
    for k in range(64):
        ref[8 * k:8 * k + 8, :] = tiles[k]


def kept_tile(ref, k):
    return ref[8 * k:8 * k + 8, :]


def dot(a, b):
    return jnp.dot(a, b, precision=HIGH, preferred_element_type=F32)


def dot_nt(a, b):
    return lax.dot_general(a, b, (((1,), (1,)), ((), ())), precision=HIGH, preferred_element_type=F32)


def kernel(rec, meta, prop_in, cov_in, kslab_in, damp, prior, filt_out, smooth_out,
           land, mland, lhs, acc, r1, hs, r2, fh, r3, ri, om, wide, slab, slab_t, brow, maps, brows, kfull, k_t,
           dsrc, dl, psrc, pr, hop_src, hop_in, start_src, start_in, msg, mail, kept, mail_tiles, d_tiles, b_tiles,
           s_rec, r_rec, s_meta, r_meta, s_k, r_k, s_d, r_d, s_p, r_p, s_1, r_1, s_i, r_i, s_2, r_2, s_3, r_3,
           s_a, r_a, s_b, r_b, s_h, r_h, s_s, r_s, s_m, r_m, l_rec, l_meta, prop, cov, kslab, l_in):
    tm, x = lax.axis_index("tm"), lax.axis_index("obs")
    z, y, core = tm // 8, (tm // 2) % 4, tm % 2
    q, xi = x // 2, x % 2
    g, i_row = place_row(y, z)
    e_me = 2 * i_row + q
    c_me = 8 * g + e_me
    j = 2 * xi + core
    lead_tm = lead_of(g)
    is_lead = jnp.logical_and(tm == lead_tm, x == 1)
    sib = tm + 1 - 2 * core
    xp = x + 1 - 2 * xi

    def remote(src, dst, ss, rs, dev):
        return pltpu.make_async_remote_copy(src_ref=src, dst_ref=dst, send_sem=ss, recv_sem=rs, device_id=dev,
                                            device_id_type=MESH)

    drains = []

    def sent(copy, when=None):
        if when is None:
            drains.append(copy.wait_send)
        else:
            drains.append(lambda: pl.when(when)(copy.wait_send))

    barrier = pltpu.get_barrier_semaphore()

    def owner_of(o):
        dq, dy, dz = o // 16, (o // 4) % 4, o % 4
        return ((z + dz) % 4, (y + dy) % 4, (q + dq) % 2, x + dq * (3 - 2 * x)), (
            ((z - dz + 4) % 4) * 8 + ((y - dy + 4) % 4) * 2 + core, x + dq * (3 - 2 * x))

    dr_y, dr_z = row_place(tm // 2)
    d_tm, d_x = dr_z * 8 + dr_y * 2 + x % 2, 2 * (tm % 2) + x // 2
    d_self = jnp.logical_and(d_tm == tm, d_x == x)

    def greet(dev):
        pl.semaphore_signal(barrier, 1, device_id=dev, device_id_type=MESH)

    def greet_source(o, carry):
        greet(owner_of(o)[1])
        return carry

    loads = [pltpu.make_async_copy(a, b, l_in.at[n])
             for n, (a, b) in enumerate(((prop_in, prop), (cov_in, cov), (kslab_in, kslab)))]
    lax.fori_loop(1, 32, greet_source, 0)
    for dev in ((tm, (x + 1) % 4), (tm, (x + 2) % 4), (tm, (x + 3) % 4), (sib, x), (sib, xp),
                (c_me, 2 * xi + core)):
        greet(dev)
    for load in loads:
        load.start()
    acc[...] = jnp.zeros_like(acc)
    pl.semaphore_wait(barrier, 37)

    def offset(m):
        return 1 + ((m - 1) * 11 + core * 15) % 31

    def record_copies(m):
        o = offset(m)
        tz, ty, tq, tx = owner_of(o)[0]
        tg, ti = place_row(ty, tz)
        c = 8 * tg + 2 * ti + tq
        dev = (tz * 8 + ty * 2 + core, tx)
        return (
            remote(rec.at[pl.ds(pl.multiple_of(c * 128, 128), 128)],
                   land.at[m // 2, pl.ds(pl.multiple_of((m % 2) * 128, 128), 128)], s_rec.at[m], r_rec.at[m], dev),
            remote(meta.at[c], mland.at[m], s_meta.at[m], r_meta.at[m], dev),
        )

    own_rec = pltpu.make_async_copy(rec.at[pl.ds(pl.multiple_of(c_me * 128, 128), 128)],
                                    land.at[0, pl.ds(0, 128)], l_rec)
    own_rec.start()
    own_meta = pltpu.make_async_copy(meta.at[c_me], mland.at[0], l_meta)
    own_meta.start()

    def send_record(m, carry):
        a, b = record_copies(m)
        b.start()
        a.start()
        return carry

    dsrc[...] = jnp.zeros_like(dsrc)
    dsrc[0:2, :] = damp[...]
    d_copy = remote(dsrc, dl, s_d.at[0], r_d.at[0], (d_tm, d_x))

    @pl.when(d_self)
    def _():
        dl[...] = dsrc[...]

    @pl.when(jnp.logical_not(d_self))
    def _():
        d_copy.start()

    sent(d_copy, jnp.logical_not(d_self))

    lax.fori_loop(1, 32, send_record, 0)

    def drain_record(m, carry):
        a, b = record_copies(m)
        a.wait_send()
        b.wait_send()
        return carry

    drains.append(lambda: lax.fori_loop(1, 32, drain_record, 0))

    for load in loads:
        load.wait()
    own_rec.wait()
    own_meta.wait()

    def wait_record(m):
        a, b = record_copies(m)
        b.wait_recv()
        a.wait_recv()

    def gram(p, carry):
        @pl.when(p > 0)
        def _():
            wait_record(2 * p)
        wait_record(2 * p + 1)
        rows = land[p]
        marks = jnp.concatenate([mland[2 * p], mland[2 * p + 1]], axis=1)
        rows_t = rows.T
        lhs[0:512, :] = rows_t * marks[2:3, :]
        lhs[512:1024, :] = rows_t * marks[3:4, :]
        lhs[1024:1040, :] = marks
        acc[...] += jnp.dot(lhs[...], rows, preferred_element_type=F32)
        return carry

    lax.fori_loop(0, 16, gram, 0)

    def first_copies(d, owner):
        return [remote(acc.at[pl.ds(d * 512 + 128 * r, 128), pl.ds(c0, w)], r1.at[d, :, pl.ds(at, w)],
                       s_1.at[2 * d + n], r_1.at[2 * d + n], (sib, x))
                for n, (r, c0, w, at) in enumerate(PARTS[owner])]

    def by_core(step):
        for own in range(2):
            pl.when(core == own)(lambda own=own: step(own))

    peers = ((sib, x), (tm, xp), (sib, xp))
    info_copies = [remote(acc.at[pl.ds(1024, 8), :], ri.at[n], s_i.at[n], r_i.at[n], peers[n]) for n in range(3)]
    def give(own):
        for d in range(2):
            for copy in first_copies(d, 1 - own):
                copy.start()

    def given(own):
        for d in range(2):
            for copy in first_copies(d, 1 - own):
                copy.wait_send()

    by_core(give)
    drains.append(lambda: by_core(given))
    for copy in info_copies:
        copy.start()
        sent(copy)
    second = [remote(hs.at[d], r2.at[d], s_2.at[d], r_2.at[d], (tm, xp)) for d in range(2)]
    third = [remote(fh.at[d], r3.at[d], s_3.at[d], r_3.at[d], (sib, x)) for d in range(2)]
    for d in range(2):
        def add(own, d=d):
            for copy in first_copies(d, own):
                copy.wait_recv()
            for r, c0, w, at in PARTS[own]:
                hs[d, :, at:at + w] = (acc[d * 512 + 128 * r:d * 512 + 128 * r + 128, c0:c0 + w]
                                       + r1[d, :, at:at + w])

        by_core(add)
        second[d].start()
        sent(second[d])
    for copy in info_copies:
        copy.wait_recv()
    info = (acc[1024:1032, :] + ri[0]) + (ri[1] + ri[2])

    @pl.when(jnp.logical_not(d_self))
    def _():
        d_copy.wait_recv()

    d_rows = dl[...]
    for d in range(2):
        keep(d_tiles.at[d], to_tiles(d_rows[d:d + 1, :]))

    wide[0:128, :] = prop[:, pl.ds(pl.multiple_of(j * 128, 128), 128)].T * d_rows[0:1, :]
    wide[128:136, :] = jnp.zeros((8, S), F32)
    for d in range(2):
        second[d].wait_recv()
        fh[d] = hs[d] + r2[d]
        third[d].start()
        sent(third[d])
        def put(own, src, d=d):
            for r, c0, w, at in PARTS[own]:
                om[d, 128 * r:128 * r + 128, c0:c0 + w] = src[d, :, at:at + w]

        by_core(lambda own: put(own, fh))
        third[d].wait_recv()
        by_core(lambda own: put(1 - own, r3))
        for r in range(1, 4):
            for c in range(r):
                om[d, 128 * r:128 * r + 128, 128 * c:128 * c + 128] = (
                    om[d, 128 * c:128 * c + 128, 128 * r:128 * r + 128].T)
        if d == 1:
            wide[...] = dot_nt(wide[...], prop[...]) * d_rows[1:2, :]
        w = wide[...]
        seen = jnp.concatenate([jnp.zeros((128, S), F32), jnp.broadcast_to(info[d:d + 1, :], (8, S))], axis=0)
        wide[...] = w - dot(dot(w, om[d]) - seen, cov[...])

    lead = (lead_tm, 1)
    slab_cols = pl.multiple_of(j * 128, 128)
    even_copy = remote(slab_t, maps.at[e_me, :, pl.ds(slab_cols, 128)], s_a.at[0], r_a.at[e_me * 4 + j], lead)
    odd_copy = remote(slab, maps.at[e_me, pl.ds(slab_cols, 128), :], s_a.at[0], r_a.at[e_me * 4 + j], lead)
    b_copy = remote(brow, brows.at[e_me], s_b.at[0], r_b.at[e_me], lead)

    @pl.when(q == 0)
    def _():
        slab_t[...] = wide[0:128, :].T

    @pl.when(q == 1)
    def _():
        slab[...] = wide[0:128, :]

    @pl.when(is_lead)
    def _():
        maps[0, :, 256:384] = slab_t[...]

    even_send = jnp.logical_and(q == 0, jnp.logical_not(is_lead))

    @pl.when(even_send)
    def _():
        even_copy.start()

    sent(even_copy, even_send)

    @pl.when(q == 1)
    def _():
        odd_copy.start()

    sent(odd_copy, q == 1)

    brow[...] = wide[128:136, :]

    @pl.when(j == 0)
    def _():
        b_copy.start()

    sent(b_copy, j == 0)

    psrc[...] = jnp.broadcast_to(prior[...], (8, 128))
    p_copy = remote(psrc, pr.at[x], s_p.at[0], r_p.at[x], (lead_of(0), 1))
    p_send = jnp.logical_and(tm == lead_of(0), x != 1)

    @pl.when(p_send)
    def _():
        p_copy.start()

    sent(p_copy, p_send)

    @pl.when(jnp.logical_and(tm == lead_of(0), x == 1))
    def _():
        pr[1] = psrc[...]

    def gain_copy(n):
        return remote(kslab, kfull.at[pl.ds(pl.multiple_of(x * 128, 128), 128)], s_k.at[n], r_k.at[n],
                      (tm, (x + n) % 4))

    def gain_in(n):
        ox = (x - n + 4) % 4
        return remote(kslab, kfull.at[pl.ds(pl.multiple_of(ox * 128, 128), 128)], s_k.at[n], r_k.at[n], (tm, xp))

    for n in range(1, 4):
        gain_copy(n).start()
        sent(gain_copy(n))
    kfull[pl.ds(pl.multiple_of(x * 128, 128), 128), :] = kslab[...]

    for n in range(1, 4):
        gain_in(n).wait_recv()
    k_t[...] = kfull[...].T

    next_g = (g + 1) % 4
    hop_copy = remote(hop_src, hop_in, s_h.at[0], r_h.at[0], (lead_of(next_g), 1))

    def start_copy(e, n):
        sy, sz = row_place(4 * g + e // 2)
        return remote(start_src.at[e], start_in, s_s.at[e * 4 + n], r_s.at[0],
                      (sz * 8 + sy * 2 + n % 2, 2 * (e % 2) + n // 2))

    @pl.when(is_lead)
    def _():
        @pl.when(g == 0)
        def _():
            for ox in (0, 2, 3):
                remote(psrc, pr.at[ox], s_p.at[0], r_p.at[ox], (sib, x)).wait_recv()
            for ox in range(4):
                hop_in[:, 128 * ox:128 * ox + 128] = pr[ox]

        for e in range(8):
            for n in range(4):
                if (e, n) == (0, 2):
                    continue
                if e % 2 == 0:
                    remote(slab_t, maps.at[e, :, pl.ds(128 * n, 128)], s_a.at[0], r_a.at[e * 4 + n],
                           (sib, x)).wait_recv()
                else:
                    remote(slab, maps.at[e, pl.ds(128 * n, 128), :], s_a.at[0], r_a.at[e * 4 + n],
                           (sib, x)).wait_recv()
            remote(brow, brows.at[e], s_b.at[0], r_b.at[e], (sib, x)).wait_recv()

        for e in range(0, 8, 2):
            keep(b_tiles.at[e // 2], to_tiles(brows[e, 0:1, :]))

        @pl.when(g > 0)
        def _():
            hop_copy.wait_recv()

        row = hop_in[0:1, :]
        for e in range(0, 8, 2):
            start_src[e] = jnp.broadcast_to(row, (8, S))
            tiles = row_times(maps.at[e], row)
            tiles = [tiles[k] + kept_tile(b_tiles.at[e // 2], k) for k in range(64)]
            row = col_times(maps.at[e + 1], tiles) + brows[e + 1, 0:1, :]
            start_src[e + 1] = jnp.broadcast_to(to_row(tiles), (8, S))
        hop_src[...] = jnp.broadcast_to(row, (8, S))

        @pl.when(g < 3)
        def _():
            hop_copy.start()

        start_in[...] = start_src[0]
        for e in range(7, -1, -1):
            for n in range(4):
                if (e, n) != (0, 2):
                    start_copy(e, n).start()

    def drain_leader():
        for e in range(8):
            for n in range(4):
                if (e, n) != (0, 2):
                    start_copy(e, n).wait_send()

        @pl.when(g < 3)
        def _():
            hop_copy.wait_send()

    drains.append(lambda: pl.when(is_lead)(drain_leader))

    @pl.when(jnp.logical_not(is_lead))
    def _():
        start_copy(0, 0).wait_recv()

    before = start_in[0:1, :]

    def day(d, ahead):
        moved = [kept_tile(d_tiles.at[d], k) * ahead[k] for k in range(64)]
        back = row_times(cov, col_times(om.at[d], moved) - info[d:d + 1, :])
        return to_row([moved[k] - back[k] for k in range(64)])

    first = day(0, row_times(prop, before))
    ahead = row_times(prop, first)
    last = day(1, ahead)
    d_first, d_last = d_rows[0:1, :], d_rows[1:2, :]
    msg[0:1, :] = first
    msg[1:2, :] = last
    msg[2:3, :] = d_last * (last - d_last * to_row(ahead))
    msg[3:4, :] = to_row(row_times(prop, last))
    msg[4:5, :] = d_first
    msg[5:6, :] = d_last
    msg[6:8, :] = jnp.zeros((2, S), F32)

    def mail_copy(n):
        return remote(msg, mail.at[c_me], s_m.at[n], r_m.at[c_me], (n, j))

    to_self = j == x

    @pl.when(to_self)
    def _():
        mail[c_me] = msg[...]

    def to_other(n):
        return jnp.logical_or(n != tm, jnp.logical_not(to_self))

    def post(n, carry):
        @pl.when(to_other(n))
        def _():
            mail_copy(n).start()
        return carry

    lax.fori_loop(0, 32, post, 0)

    def drain_post(n, carry):
        @pl.when(to_other(n))
        def _():
            mail_copy(n).wait_send()
        return carry

    drains.append(lambda: lax.fori_loop(0, 32, drain_post, 0))

    def wait_mail(c):
        @pl.when(jnp.logical_not(jnp.logical_and(to_self, c == c_me)))
        def _():
            remote(msg, mail.at[c], s_m.at[0], r_m.at[c], (sib, x)).wait_recv()

    own_cols = pl.ds(pl.multiple_of(x * 128, 128), 128)

    def expand(c, carry):
        wait_mail(c)
        keep(mail_tiles.at[c, 0], to_tiles(mail[c, 5:6, :]))
        keep(mail_tiles.at[c, 1], to_tiles(mail[c, 2:3, :]))
        return carry

    lax.fori_loop(tm, 32, expand, 0)

    def back(c, state, damp_next):
        gap = damp_next * (state - damp_next * mail[c, 3:4, :])
        later = row_times(kfull, gap)
        scale, shift = mail_tiles.at[c, 0], mail_tiles.at[c, 1]
        gaps = [kept_tile(scale, k) * later[k] + kept_tile(shift, k) for k in range(64)]
        return mail[c, 0:1, :] + col_times(k_t, gaps), later

    def back_step(n, carry):
        state, damp_next = carry
        c = 31 - n
        return back(c, state, damp_next)[0], mail[c, 4:5, :]

    zero = jnp.zeros((1, S), F32)
    state, damp_next = lax.fori_loop(0, 31 - tm, back_step, (zero, zero))
    state, later = back(tm, state, damp_next)
    kept[0:1, :] = state
    kept[1:2, :] = mail[tm, 1:2, :] + to_row(later)
    smooth_out[...] = kept[0:2, own_cols]
    filt_out[...] = mail[tm, 0:2, own_cols]

    def drain_mail(n, carry):
        wait_mail(n)
        return carry

    lax.fori_loop(0, tm, drain_mail, 0)
    for drain in drains:
        drain()


def hand_out(filt, smooth, filt_out, smooth_out):
    filt_out[...] = filt[...]
    smooth_out[...] = smooth[...]


def local(records, obs_values, block_day, block_count, propagator_matrix, analysis_cov, unattenuated_multiplier,
          damping, prior_mean):
    slot = lax.broadcasted_iota(jnp.int32, (32, 16, 128), 2)
    part = lax.broadcasted_iota(jnp.int32, (32, 16, 128), 1)
    held = jnp.logical_and(slot < block_count[:, None, None], block_day[:, None, None] == part % 2)
    held = jnp.logical_and(held, part < 4)
    values = jnp.where(part < 2, obs_values.reshape(32, 1, 128), jnp.ones((), BF16))
    meta = jnp.where(held, values, jnp.zeros((), BF16))
    vmem = pl.BlockSpec(memory_space=pltpu.VMEM)
    hbm = pl.BlockSpec(memory_space=pl.ANY)
    dma = pltpu.SemaphoreType.DMA
    results = pl.pallas_call(
        kernel,
        out_shape=(jax.ShapeDtypeStruct((2, 128), F32), jax.ShapeDtypeStruct((2, 128), F32)),
        in_specs=[hbm] * 5 + [vmem] * 2,
        out_specs=(vmem, vmem),
        scratch_shapes=[
            pltpu.VMEM((16, 256, S), BF16),
            pltpu.VMEM((32, 16, 128), BF16),
            pltpu.VMEM((1040, 256), BF16),
            pltpu.VMEM((1040, S), F32),
            pltpu.VMEM((2, 128, 640), F32),
            pltpu.VMEM((2, 128, 640), F32),
            pltpu.VMEM((2, 128, 640), F32),
            pltpu.VMEM((2, 128, 640), F32),
            pltpu.VMEM((2, 128, 640), F32),
            pltpu.VMEM((3, 8, S), F32),
            pltpu.VMEM((2, S, S), F32),
            pltpu.VMEM((136, S), F32),
            pltpu.VMEM((128, S), F32),
            pltpu.VMEM((S, 128), F32),
            pltpu.VMEM((8, S), F32),
            pltpu.VMEM((8, S, S), F32),
            pltpu.VMEM((8, 8, S), F32),
            pltpu.VMEM((S, S), F32),
            pltpu.VMEM((S, S), F32),
            pltpu.VMEM((8, S), F32),
            pltpu.VMEM((8, S), F32),
            pltpu.VMEM((8, 128), F32),
            pltpu.VMEM((4, 8, 128), F32),
            pltpu.VMEM((8, S), F32),
            pltpu.VMEM((8, S), F32),
            pltpu.VMEM((8, 8, S), F32),
            pltpu.VMEM((8, S), F32),
            pltpu.VMEM((8, S), F32),
            pltpu.VMEM((32, 8, S), F32),
            pltpu.VMEM((8, S), F32),
            pltpu.VMEM((32, 2, S, 128), F32),
            pltpu.VMEM((2, S, 128), F32),
            pltpu.VMEM((4, S, 128), F32),
            dma((32,)), dma((32,)), dma((32,)), dma((32,)),
            dma((4,)), dma((4,)), dma((1,)), dma((1,)), dma((1,)), dma((4,)),
            dma((4,)), dma((4,)), dma((3,)), dma((3,)), dma((2,)), dma((2,)), dma((2,)), dma((2,)),
            dma((1,)), dma((32,)), dma((1,)), dma((8,)), dma((1,)), dma((1,)),
            dma((32,)), dma((1,)), dma((32,)), dma((32,)), dma, dma,
            pltpu.VMEM((S, S), F32), pltpu.VMEM((S, S), F32), pltpu.VMEM((128, S), F32), dma((3,)),
        ],
        compiler_params=pltpu.CompilerParams(collective_id=0, has_side_effects=True, vmem_limit_bytes=56 << 20),
        cost_estimate=pl.CostEstimate(flops=10**10, bytes_accessed=10**8, transcendentals=0),
    )(records, meta, propagator_matrix, analysis_cov, unattenuated_multiplier, damping, prior_mean.reshape(1, 128))
    return pl.pallas_call(
        hand_out,
        out_shape=(jax.ShapeDtypeStruct((2, 128), F32), jax.ShapeDtypeStruct((2, 128), F32)),
        in_specs=[vmem, vmem],
        out_specs=(vmem, vmem),
    )(*results)


def solution(mesh):
    return jax.shard_map(
        local,
        mesh=mesh,
        in_specs=(
            P(("tm", "obs"), None),
            P(("tm", "obs")),
            P(("tm", "obs")),
            P(("tm", "obs")),
            P(),
            P(),
            P("obs", None),
            P("tm", None),
            P("obs"),
        ),
        out_specs=(P("tm", "obs"), P("tm", "obs")),
        check_vma=False,
    )
```

```python
import jax
import jax.numpy as jnp
from jax import lax
from jax.experimental import pallas as pl
from jax.experimental.pallas import tpu as pltpu
from jax.sharding import PartitionSpec as P

MESH = pl.DeviceIdType.MESH
F32 = jnp.float32
BF16 = jnp.bfloat16
S = 512


def row_place(r):
    g, i = r // 4, r % 4
    im = i % 3
    return (2 * (g // 2) + im * (im + 1) // 2) % 4, g + (i // 3) * (3 - 2 * g)


def place_row(y, z):
    odd = y % 2
    extra = (1 - odd) * ((y // 2 + z // 2) % 2)
    g = z + extra * (3 - 2 * z)
    return g, odd * (1 + ((y - 2 * (z // 2) + 4) % 4) // 2) + 3 * extra


def lead_of(g):
    return g * 8 + g // 2 * 4


PARTS = (((0, 0, 512, 0), (3, 384, 128, 512)), ((1, 128, 384, 0), (2, 256, 256, 384)))


def row_times(ref, row):
    wide = jnp.broadcast_to(row, (8, S))
    tiles = []
    for k in range(0, S, 8):
        t = [ref[k:k + 8, n:n + 128] * wide[:, n:n + 128] for n in range(0, S, 128)]
        tiles.append(jnp.broadcast_to(jnp.sum((t[0] + t[1]) + (t[2] + t[3]), axis=1, keepdims=True), (8, 128)))
    return tiles


def col_times(ref, tiles):
    out = []
    for n in range(0, S, 128):
        total = [None] * 4
        for k in range(64):
            p = ref[8 * k:8 * k + 8, n:n + 128] * tiles[k]
            total[k % 4] = p if total[k % 4] is None else total[k % 4] + p
        out.append(jnp.sum((total[0] + total[1]) + (total[2] + total[3]), axis=0, keepdims=True))
    return jnp.concatenate(out, axis=1)


def diagonals():
    lead = lax.broadcasted_iota(jnp.int32, (8, 128), 1) - lax.broadcasted_iota(jnp.int32, (8, 128), 0)
    return [lead == 8 * k for k in range(16)]


def to_row(tiles):
    marks = diagonals()
    out = []
    for n in range(4):
        picked = [jnp.where(marks[k], tiles[16 * n + k], 0.0) for k in range(16)]
        while len(picked) > 1:
            picked = [picked[k] + picked[k + 1] for k in range(0, len(picked), 2)]
        out.append(jnp.sum(picked[0], axis=0, keepdims=True))
    return jnp.concatenate(out, axis=1)


def to_tiles(row):
    marks = diagonals()
    tiles = []
    for n in range(4):
        part = jnp.broadcast_to(row[:, 128 * n:128 * n + 128], (8, 128))
        for k in range(16):
            tiles.append(jnp.broadcast_to(
                jnp.sum(jnp.where(marks[k], part, 0.0), axis=1, keepdims=True), (8, 128)))
    return tiles


def keep(ref, tiles):
    for k in range(64):
        ref[8 * k:8 * k + 8, :] = tiles[k]


def kept_tile(ref, k):
    return ref[8 * k:8 * k + 8, :]


def parts_of(a):
    high = a.astype(BF16)
    return high, (a - high.astype(F32)).astype(BF16)


def dot(a, parts):
    high, low = parts_of(a)
    b_high, b_low = parts

    def product(u, v):
        return jnp.dot(u, v, preferred_element_type=F32)

    return product(high, b_high) + (product(high, b_low) + product(low, b_high))


def kernel(rec, values, days, counts, prop_in, cov_in, kslab_in, damp, prior, filt_out, smooth_out,
           land, mland, lhs, acc, r1, hs, r2, fh, r3, ri, om, wide, slab, slab_t, brow, maps, brows, kfull, k_t,
           dsrc, dl, psrc, pr, hop_src, hop_in, start_src, start_in, msg, mail, kept, mail_tiles, d_tiles, b_tiles,
           s_rec, r_rec, s_meta, r_meta, s_k, r_k, s_d, r_d, s_p, r_p, s_1, r_1, s_i, r_i, s_2, r_2, s_3, r_3,
           s_a, r_a, s_b, r_b, s_h, r_h, s_s, r_s, s_m, r_m, l_rec, prop, cov, kslab, l_in, meta, plain, s_w, r_w, s_r, pt_parts, c_parts):
    tm, x = lax.axis_index("tm"), lax.axis_index("obs")
    z, y, core = tm // 8, (tm // 2) % 4, tm % 2
    q, xi = x // 2, x % 2
    g, i_row = place_row(y, z)
    e_me = 2 * i_row + q
    c_me = 8 * g + e_me
    j = 2 * xi + core
    lead_tm = lead_of(g)
    is_lead = jnp.logical_and(tm == lead_tm, x == 1)
    sib = tm + 1 - 2 * core
    xp = x + 1 - 2 * xi

    def remote(src, dst, ss, rs, dev):
        return pltpu.make_async_remote_copy(src_ref=src, dst_ref=dst, send_sem=ss, recv_sem=rs, device_id=dev,
                                            device_id_type=MESH)

    drains = []

    def sent(copy, when=None):
        if when is None:
            drains.append(copy.wait_send)
        else:
            drains.append(lambda: pl.when(when)(copy.wait_send))

    barrier = pltpu.get_barrier_semaphore()

    def owner_of(o):
        dq, dy, dz = o // 16, (o // 4) % 4, o % 4
        return ((z + dz) % 4, (y + dy) % 4, (q + dq) % 2, x + dq * (3 - 2 * x)), (
            ((z - dz + 4) % 4) * 8 + ((y - dy + 4) % 4) * 2 + core, x + dq * (3 - 2 * x))

    dr_y, dr_z = row_place(tm // 2)
    d_tm, d_x = dr_z * 8 + dr_y * 2 + x % 2, 2 * (tm % 2) + x // 2
    d_self = jnp.logical_and(d_tm == tm, d_x == x)

    def greet(dev):
        pl.semaphore_signal(barrier, 1, device_id=dev, device_id_type=MESH)

    def greet_source(o, carry):
        greet(owner_of(o)[1])
        return carry

    loads = [pltpu.make_async_copy(a, b, l_in.at[n])
             for n, (a, b) in enumerate(((prop_in, prop), (cov_in, cov), (kslab_in, kslab)))]
    lax.fori_loop(1, 32, greet_source, 0)
    for dev in ((tm, (x + 1) % 4), (tm, (x + 2) % 4), (tm, (x + 3) % 4), (sib, x), (sib, xp),
                (c_me, 2 * xi + core)):
        greet(dev)
    for load in loads:
        load.start()
    slot = lax.broadcasted_iota(jnp.int32, (16, 128), 1)
    part = lax.broadcasted_iota(jnp.int32, (16, 128), 0)
    plain[...] = values[...].astype(F32)

    def mark(c):
        held = jnp.logical_and(jnp.logical_and(slot < counts[c], part % 2 == days[c]), part < 4)
        filled = jnp.where(part < 2, jnp.broadcast_to(plain[pl.ds(c, 1), :], (16, 128)), 1.0)
        return jnp.where(held, filled, 0.0).astype(BF16)

    mland[0] = mark(c_me)
    acc[...] = jnp.zeros_like(acc)
    pl.semaphore_wait(barrier, 37)

    def offset(m):
        return 1 + ((m - 1) * 11 + core * 15) % 31

    def record_copies(m):
        o = offset(m)
        tz, ty, tq, tx = owner_of(o)[0]
        tg, ti = place_row(ty, tz)
        c = 8 * tg + 2 * ti + tq
        dev = (tz * 8 + ty * 2 + core, tx)
        return c, (
            remote(rec.at[pl.ds(pl.multiple_of(c * 128, 128), 128)],
                   land.at[m // 2, pl.ds(pl.multiple_of((m % 2) * 128, 128), 128)], s_rec.at[m], r_rec.at[m], dev),
            remote(meta.at[c], mland.at[m], s_meta.at[m], r_meta.at[m], dev),
        )

    own_rec = pltpu.make_async_copy(rec.at[pl.ds(pl.multiple_of(c_me * 128, 128), 128)],
                                    land.at[0, pl.ds(0, 128)], l_rec)
    own_rec.start()
    def send_record(m, carry):
        c, (a, b) = record_copies(m)
        a.start()
        meta[c] = mark(c)
        b.start()
        return carry

    dsrc[...] = jnp.zeros_like(dsrc)
    dsrc[0:2, :] = damp[...]
    d_copy = remote(dsrc, dl, s_d.at[0], r_d.at[0], (d_tm, d_x))

    @pl.when(d_self)
    def _():
        dl[...] = dsrc[...]

    @pl.when(jnp.logical_not(d_self))
    def _():
        d_copy.start()

    sent(d_copy, jnp.logical_not(d_self))

    lax.fori_loop(1, 32, send_record, 0)
    loads[2].wait()
    def gain_rows(ox, half):
        return pl.ds(pl.multiple_of(ox * 128 + half * 64, 64), 64)

    half_slab = kslab.at[pl.ds(pl.multiple_of(core * 64, 64), 64)]

    def gain_copy(n, ox):
        return remote(half_slab, kfull.at[gain_rows(ox, core)], s_k.at[n], r_k.at[n], (tm, (x + n) % 4))

    def gain_swap(n, half):
        rows = gain_rows((x - n + 4) % 4, half)
        return remote(kfull.at[rows], kfull.at[rows], s_w.at[n], r_w.at[n], (sib, x))

    for n in range(1, 4):
        gain_copy(n, x).start()
        sent(gain_copy(n, x))
    kfull[pl.ds(pl.multiple_of(x * 128, 128), 128), :] = kslab[...]

    def drain_record(m, carry):
        a, b = record_copies(m)[1]
        a.wait_send()
        b.wait_send()
        return carry

    drains.append(lambda: lax.fori_loop(1, 32, drain_record, 0))

    for load in loads[:2]:
        load.wait()
    pt_parts[0], pt_parts[1] = parts_of(prop[...].T)
    c_parts[0], c_parts[1] = parts_of(cov[...])
    own_rec.wait()

    def wait_record(m):
        a, b = record_copies(m)[1]
        b.wait_recv()
        a.wait_recv()

    def gram(p, carry):
        @pl.when(p > 0)
        def _():
            wait_record(2 * p)
        wait_record(2 * p + 1)
        rows = land[p]
        marks = jnp.concatenate([mland[2 * p], mland[2 * p + 1]], axis=1)
        rows_t = rows.T
        lhs[0:512, :] = rows_t * marks[2:3, :]
        lhs[512:1024, :] = rows_t * marks[3:4, :]
        lhs[1024:1040, :] = marks
        acc[...] += jnp.dot(lhs[...], rows, preferred_element_type=F32)
        return carry

    lax.fori_loop(0, 16, gram, 0)

    def first_copies(d, owner):
        return [remote(acc.at[pl.ds(d * 512 + 128 * r, 128), pl.ds(c0, w)], r1.at[d, :, pl.ds(at, w)],
                       s_1.at[2 * d + n], r_1.at[2 * d + n], (sib, x))
                for n, (r, c0, w, at) in enumerate(PARTS[owner])]

    def by_core(step):
        for own in range(2):
            pl.when(core == own)(lambda own=own: step(own))

    peers = ((sib, x), (tm, xp), (sib, xp))
    info_copies = [remote(acc.at[pl.ds(1024, 8), :], ri.at[n], s_i.at[n], r_i.at[n], peers[n]) for n in range(3)]
    def give(own):
        for d in range(2):
            for copy in first_copies(d, 1 - own):
                copy.start()

    def given(own):
        for d in range(2):
            for copy in first_copies(d, 1 - own):
                copy.wait_send()

    by_core(give)
    drains.append(lambda: by_core(given))
    for copy in info_copies:
        copy.start()
        sent(copy)
    second = [remote(hs.at[d], r2.at[d], s_2.at[d], r_2.at[d], (tm, xp)) for d in range(2)]
    third = [remote(fh.at[d], r3.at[d], s_3.at[d], r_3.at[d], (sib, x)) for d in range(2)]
    for d in range(2):
        def add(own, d=d):
            for copy in first_copies(d, own):
                copy.wait_recv()
            for r, c0, w, at in PARTS[own]:
                hs[d, :, at:at + w] = (acc[d * 512 + 128 * r:d * 512 + 128 * r + 128, c0:c0 + w]
                                       + r1[d, :, at:at + w])

        by_core(add)
        second[d].start()
        sent(second[d])
    for copy in info_copies:
        copy.wait_recv()
    info = (acc[1024:1032, :] + ri[0]) + (ri[1] + ri[2])

    @pl.when(jnp.logical_not(d_self))
    def _():
        d_copy.wait_recv()

    d_rows = dl[...]
    for d in range(2):
        keep(d_tiles.at[d], to_tiles(d_rows[d:d + 1, :]))

    wide[0:128, :] = prop[:, pl.ds(pl.multiple_of(j * 128, 128), 128)].T * d_rows[0:1, :]
    wide[128:136, :] = jnp.zeros((8, S), F32)
    for d in range(2):
        second[d].wait_recv()
        fh[d] = hs[d] + r2[d]
        third[d].start()
        sent(third[d])
        def put(own, src, d=d):
            for r, c0, w, at in PARTS[own]:
                om[d, 128 * r:128 * r + 128, c0:c0 + w] = src[d, :, at:at + w]

        by_core(lambda own: put(own, fh))
        third[d].wait_recv()
        by_core(lambda own: put(1 - own, r3))
        for r in range(1, 4):
            for c in range(r):
                om[d, 128 * r:128 * r + 128, 128 * c:128 * c + 128] = (
                    om[d, 128 * c:128 * c + 128, 128 * r:128 * r + 128].T)
        if d == 1:
            wide[...] = dot(wide[...], (pt_parts[0], pt_parts[1])) * d_rows[1:2, :]
        w = wide[...]
        seen = jnp.concatenate([jnp.zeros((128, S), F32), jnp.broadcast_to(info[d:d + 1, :], (8, S))], axis=0)
        wide[...] = w - dot(dot(w, parts_of(om[d])) - seen, (c_parts[0], c_parts[1]))

    lead = (lead_tm, 1)
    by_row = jnp.logical_and(xi == 0, (1 - q) * (i_row + 1) // 2 % 2 + q * i_row // 3 == 1)
    to_lead = (lead_tm + jnp.where(by_row, core, 0), jnp.where(by_row, x, 1))
    slab_cols = pl.multiple_of(j * 128, 128)
    even_copy = remote(slab_t, maps.at[e_me, :, pl.ds(slab_cols, 128)], s_a.at[0], r_a.at[e_me * 4 + j], to_lead)
    odd_copy = remote(slab, maps.at[e_me, pl.ds(slab_cols, 128), :], s_a.at[0], r_a.at[e_me * 4 + j], to_lead)
    b_copy = remote(brow, brows.at[e_me], s_b.at[0], r_b.at[e_me], lead)

    @pl.when(q == 0)
    def _():
        slab_t[...] = wide[0:128, :].T

    @pl.when(q == 1)
    def _():
        slab[...] = wide[0:128, :]

    @pl.when(is_lead)
    def _():
        maps[0, :, 256:384] = slab_t[...]

    even_send = jnp.logical_and(q == 0, jnp.logical_not(is_lead))

    @pl.when(even_send)
    def _():
        even_copy.start()

    sent(even_copy, even_send)

    @pl.when(q == 1)
    def _():
        odd_copy.start()

    sent(odd_copy, q == 1)

    brow[...] = wide[128:136, :]

    @pl.when(j == 0)
    def _():
        b_copy.start()

    sent(b_copy, j == 0)

    psrc[...] = jnp.broadcast_to(prior[...], (8, 128))
    p_copy = remote(psrc, pr.at[x], s_p.at[0], r_p.at[x], (lead_of(0), 1))
    p_send = jnp.logical_and(tm == lead_of(0), x != 1)

    @pl.when(p_send)
    def _():
        p_copy.start()

    sent(p_copy, p_send)

    @pl.when(jnp.logical_and(tm == lead_of(0), x == 1))
    def _():
        pr[1] = psrc[...]

    def pass_on(e):
        if e % 2 == 0:
            place = maps.at[e, :, pl.ds(slab_cols, 128)]
        else:
            place = maps.at[e, pl.ds(slab_cols, 128), :]
        return remote(place, place, s_r.at[e], r_a.at[e * 4 + j], lead)

    in_middle = jnp.logical_and(i_row == 0, xi == 0)
    for at_q, passed in ((0, (2, 4)), (1, (7,))):
        relays = jnp.logical_and(in_middle, q == at_q)

        @pl.when(relays)
        def _(passed=passed):
            for e in passed:
                pass_on(e).wait_recv()
                pass_on(e).start()

        for e in passed:
            sent(pass_on(e), relays)

    for n in range(1, 4):
        gain_copy(n, (x - n + 4) % 4).wait_recv()
        gain_swap(n, core).start()
        sent(gain_swap(n, core))
    for n in range(1, 4):
        gain_swap(n, 1 - core).wait_recv()
    k_t[...] = kfull[...].T

    to_self = j == x

    def wait_mail(c):
        @pl.when(jnp.logical_not(jnp.logical_and(to_self, c == c_me)))
        def _():
            remote(msg, mail.at[c], s_m.at[0], r_m.at[c], (sib, x)).wait_recv()

    def expand(c, carry):
        wait_mail(c)
        keep(mail_tiles.at[c, 0], to_tiles(mail[c, 5:6, :]))
        keep(mail_tiles.at[c, 1], to_tiles(mail[c, 2:3, :]))
        return carry

    early_end = jnp.maximum(tm, 8 * (g - 1))
    early_lead = jnp.maximum(tm, 8 * (g - 2))

    next_g = (g + 1) % 4
    hop_copy = remote(hop_src, hop_in, s_h.at[0], r_h.at[0], (lead_of(next_g), 1))

    def start_copy(e, n):
        sy, sz = row_place(4 * g + e // 2)
        return remote(start_src.at[e], start_in, s_s.at[e * 4 + n], r_s.at[0],
                      (sz * 8 + sy * 2 + n % 2, 2 * (e % 2) + n // 2))

    @pl.when(is_lead)
    def _():
        @pl.when(g == 0)
        def _():
            for ox in (0, 2, 3):
                remote(psrc, pr.at[ox], s_p.at[0], r_p.at[ox], (sib, x)).wait_recv()
            for ox in range(4):
                hop_in[:, 128 * ox:128 * ox + 128] = pr[ox]

        for e in range(8):
            for n in range(4):
                if (e, n) == (0, 2):
                    continue
                if e % 2 == 0:
                    remote(slab_t, maps.at[e, :, pl.ds(128 * n, 128)], s_a.at[0], r_a.at[e * 4 + n],
                           (sib, x)).wait_recv()
                else:
                    remote(slab, maps.at[e, pl.ds(128 * n, 128), :], s_a.at[0], r_a.at[e * 4 + n],
                           (sib, x)).wait_recv()
            remote(brow, brows.at[e], s_b.at[0], r_b.at[e], (sib, x)).wait_recv()

        for e in range(0, 8, 2):
            keep(b_tiles.at[e // 2], to_tiles(brows[e, 0:1, :]))

        lax.fori_loop(tm, early_lead, expand, 0)

        @pl.when(g > 0)
        def _():
            hop_copy.wait_recv()

        row = hop_in[0:1, :]
        for e in range(0, 8, 2):
            start_src[e] = jnp.broadcast_to(row, (8, S))
            tiles = row_times(maps.at[e], row)
            tiles = [tiles[k] + kept_tile(b_tiles.at[e // 2], k) for k in range(64)]
            row = col_times(maps.at[e + 1], tiles) + brows[e + 1, 0:1, :]
            start_src[e + 1] = jnp.broadcast_to(to_row(tiles), (8, S))
        hop_src[...] = jnp.broadcast_to(row, (8, S))

        @pl.when(g < 3)
        def _():
            hop_copy.start()

        start_in[...] = start_src[0]
        for e in range(7, -1, -1):
            for n in range(4):
                if (e, n) != (0, 2):
                    start_copy(e, n).start()

    def drain_leader():
        for e in range(8):
            for n in range(4):
                if (e, n) != (0, 2):
                    start_copy(e, n).wait_send()

        @pl.when(g < 3)
        def _():
            hop_copy.wait_send()

    drains.append(lambda: pl.when(is_lead)(drain_leader))

    lax.fori_loop(jnp.where(is_lead, early_lead, tm), early_end, expand, 0)

    @pl.when(jnp.logical_not(is_lead))
    def _():
        start_copy(0, 0).wait_recv()

    before = start_in[0:1, :]

    def day(d, ahead):
        moved = [kept_tile(d_tiles.at[d], k) * ahead[k] for k in range(64)]
        back = row_times(cov, col_times(om.at[d], moved) - info[d:d + 1, :])
        return to_row([moved[k] - back[k] for k in range(64)])

    first = day(0, row_times(prop, before))
    ahead = row_times(prop, first)
    last = day(1, ahead)
    d_first, d_last = d_rows[0:1, :], d_rows[1:2, :]
    msg[0:1, :] = first
    msg[1:2, :] = last
    msg[2:3, :] = d_last * (last - d_last * to_row(ahead))
    msg[3:4, :] = to_row(row_times(prop, last))
    msg[4:5, :] = d_first
    msg[5:6, :] = d_last
    msg[6:8, :] = jnp.zeros((2, S), F32)

    def mail_copy(n):
        return remote(msg, mail.at[c_me], s_m.at[n], r_m.at[c_me], (n, j))

    @pl.when(to_self)
    def _():
        mail[c_me] = msg[...]

    def to_other(n):
        return jnp.logical_or(n != tm, jnp.logical_not(to_self))

    def post(n, carry):
        @pl.when(to_other(n))
        def _():
            mail_copy(n).start()
        return carry

    lax.fori_loop(0, 32, post, 0)

    def drain_post(n, carry):
        @pl.when(to_other(n))
        def _():
            mail_copy(n).wait_send()
        return carry

    drains.append(lambda: lax.fori_loop(0, 32, drain_post, 0))

    own_cols = pl.ds(pl.multiple_of(x * 128, 128), 128)

    lax.fori_loop(early_end, 32, expand, 0)

    def back(c, state, damp_next):
        gap = damp_next * (state - damp_next * mail[c, 3:4, :])
        later = row_times(kfull, gap)
        scale, shift = mail_tiles.at[c, 0], mail_tiles.at[c, 1]
        gaps = [kept_tile(scale, k) * later[k] + kept_tile(shift, k) for k in range(64)]
        return mail[c, 0:1, :] + col_times(k_t, gaps), later

    def back_step(n, carry):
        state, damp_next = carry
        c = 31 - n
        return back(c, state, damp_next)[0], mail[c, 4:5, :]

    zero = jnp.zeros((1, S), F32)
    state, damp_next = lax.fori_loop(0, 31 - tm, back_step, (zero, zero))
    state, later = back(tm, state, damp_next)
    kept[0:1, :] = state
    kept[1:2, :] = mail[tm, 1:2, :] + to_row(later)
    smooth_out[...] = kept[0:2, own_cols]
    filt_out[...] = mail[tm, 0:2, own_cols]

    def drain_mail(n, carry):
        wait_mail(n)
        return carry

    lax.fori_loop(0, tm, drain_mail, 0)
    for drain in drains:
        drain()


def hand_out(filt, smooth, filt_out, smooth_out):
    filt_out[...] = filt[...]
    smooth_out[...] = smooth[...]


def local(records, obs_values, block_day, block_count, propagator_matrix, analysis_cov, unattenuated_multiplier,
          damping, prior_mean):
    vmem = pl.BlockSpec(memory_space=pltpu.VMEM)
    hbm = pl.BlockSpec(memory_space=pl.ANY)
    smem = pl.BlockSpec(memory_space=pltpu.SMEM)
    dma = pltpu.SemaphoreType.DMA
    results = pl.pallas_call(
        kernel,
        out_shape=(jax.ShapeDtypeStruct((2, 128), F32), jax.ShapeDtypeStruct((2, 128), F32)),
        in_specs=[hbm, vmem, smem, smem] + [hbm] * 3 + [vmem] * 2,
        out_specs=(vmem, vmem),
        scratch_shapes=[
            pltpu.VMEM((16, 256, S), BF16),
            pltpu.VMEM((32, 16, 128), BF16),
            pltpu.VMEM((1040, 256), BF16),
            pltpu.VMEM((1040, S), F32),
            pltpu.VMEM((2, 128, 640), F32),
            pltpu.VMEM((2, 128, 640), F32),
            pltpu.VMEM((2, 128, 640), F32),
            pltpu.VMEM((2, 128, 640), F32),
            pltpu.VMEM((2, 128, 640), F32),
            pltpu.VMEM((3, 8, S), F32),
            pltpu.VMEM((2, S, S), F32),
            pltpu.VMEM((136, S), F32),
            pltpu.VMEM((128, S), F32),
            pltpu.VMEM((S, 128), F32),
            pltpu.VMEM((8, S), F32),
            pltpu.VMEM((8, S, S), F32),
            pltpu.VMEM((8, 8, S), F32),
            pltpu.VMEM((S, S), F32),
            pltpu.VMEM((S, S), F32),
            pltpu.VMEM((8, S), F32),
            pltpu.VMEM((8, S), F32),
            pltpu.VMEM((8, 128), F32),
            pltpu.VMEM((4, 8, 128), F32),
            pltpu.VMEM((8, S), F32),
            pltpu.VMEM((8, S), F32),
            pltpu.VMEM((8, 8, S), F32),
            pltpu.VMEM((8, S), F32),
            pltpu.VMEM((8, S), F32),
            pltpu.VMEM((32, 8, S), F32),
            pltpu.VMEM((8, S), F32),
            pltpu.VMEM((32, 2, S, 128), F32),
            pltpu.VMEM((2, S, 128), F32),
            pltpu.VMEM((4, S, 128), F32),
            dma((32,)), dma((32,)), dma((32,)), dma((32,)),
            dma((4,)), dma((4,)), dma((1,)), dma((1,)), dma((1,)), dma((4,)),
            dma((4,)), dma((4,)), dma((3,)), dma((3,)), dma((2,)), dma((2,)), dma((2,)), dma((2,)),
            dma((1,)), dma((32,)), dma((1,)), dma((8,)), dma((1,)), dma((1,)),
            dma((32,)), dma((1,)), dma((32,)), dma((32,)), dma,
            pltpu.VMEM((S, S), F32), pltpu.VMEM((S, S), F32), pltpu.VMEM((128, S), F32), dma((3,)),
            pltpu.VMEM((32, 16, 128), BF16),
            pltpu.VMEM((32, 128), F32),
            dma((4,)), dma((4,)), dma((8,)),
            pltpu.VMEM((2, S, S), BF16), pltpu.VMEM((2, S, S), BF16),
        ],
        compiler_params=pltpu.CompilerParams(collective_id=0, has_side_effects=True, vmem_limit_bytes=56 << 20),
        cost_estimate=pl.CostEstimate(flops=10**10, bytes_accessed=10**8, transcendentals=0),
    )(records, obs_values.reshape(32, 128), block_day, block_count, propagator_matrix, analysis_cov, unattenuated_multiplier, damping, prior_mean.reshape(1, 128))
    return pl.pallas_call(
        hand_out,
        out_shape=(jax.ShapeDtypeStruct((2, 128), F32), jax.ShapeDtypeStruct((2, 128), F32)),
        in_specs=[vmem, vmem],
        out_specs=(vmem, vmem),
    )(*results)


def solution(mesh):
    return jax.shard_map(
        local,
        mesh=mesh,
        in_specs=(
            P(("tm", "obs"), None),
            P(("tm", "obs")),
            P(("tm", "obs")),
            P(("tm", "obs")),
            P(),
            P(),
            P("obs", None),
            P("tm", None),
            P("obs"),
        ),
        out_specs=(P("tm", "obs"), P("tm", "obs")),
        check_vma=False,
    )
```

```python
import jax
import jax.numpy as jnp
from jax import lax
from jax.experimental import pallas as pl
from jax.experimental.pallas import tpu as pltpu
from jax.sharding import PartitionSpec as P

MESH = pl.DeviceIdType.MESH
F32 = jnp.float32
BF16 = jnp.bfloat16
S = 512


def row_place(r):
    g, i = r // 4, r % 4
    im = i % 3
    return (2 * (g // 2) + im * (im + 1) // 2) % 4, g + (i // 3) * (3 - 2 * g)


def place_row(y, z):
    odd = y % 2
    extra = (1 - odd) * ((y // 2 + z // 2) % 2)
    g = z + extra * (3 - 2 * z)
    return g, odd * (1 + ((y - 2 * (z // 2) + 4) % 4) // 2) + 3 * extra


def lead_of(g):
    return g * 8 + g // 2 * 4


PARTS = (((0, 0, 512, 0), (3, 384, 128, 512)), ((1, 128, 384, 0), (2, 256, 256, 384)))


def row_times(ref, row):
    wide = jnp.broadcast_to(row, (8, S))
    tiles = []
    for k in range(0, S, 8):
        t = [ref[k:k + 8, n:n + 128] * wide[:, n:n + 128] for n in range(0, S, 128)]
        tiles.append(jnp.broadcast_to(jnp.sum((t[0] + t[1]) + (t[2] + t[3]), axis=1, keepdims=True), (8, 128)))
    return tiles


def col_times(ref, tiles):
    out = []
    for n in range(0, S, 128):
        total = [None] * 4
        for k in range(64):
            p = ref[8 * k:8 * k + 8, n:n + 128] * tiles[k]
            total[k % 4] = p if total[k % 4] is None else total[k % 4] + p
        out.append(jnp.sum((total[0] + total[1]) + (total[2] + total[3]), axis=0, keepdims=True))
    return jnp.concatenate(out, axis=1)


def diagonals():
    lead = lax.broadcasted_iota(jnp.int32, (8, 128), 1) - lax.broadcasted_iota(jnp.int32, (8, 128), 0)
    return [lead == 8 * k for k in range(16)]


def to_row(tiles):
    marks = diagonals()
    out = []
    for n in range(4):
        picked = [jnp.where(marks[k], tiles[16 * n + k], 0.0) for k in range(16)]
        while len(picked) > 1:
            picked = [picked[k] + picked[k + 1] for k in range(0, len(picked), 2)]
        out.append(jnp.sum(picked[0], axis=0, keepdims=True))
    return jnp.concatenate(out, axis=1)


def to_tiles(row):
    marks = diagonals()
    tiles = []
    for n in range(4):
        part = jnp.broadcast_to(row[:, 128 * n:128 * n + 128], (8, 128))
        for k in range(16):
            tiles.append(jnp.broadcast_to(
                jnp.sum(jnp.where(marks[k], part, 0.0), axis=1, keepdims=True), (8, 128)))
    return tiles


def keep(ref, tiles):
    for k in range(64):
        ref[8 * k:8 * k + 8, :] = tiles[k]


def kept_tile(ref, k):
    return ref[8 * k:8 * k + 8, :]


def parts_of(a):
    high = a.astype(BF16)
    return high, (a - high.astype(F32)).astype(BF16)


def dot(a, parts):
    high, low = parts_of(a)
    b_high, b_low = parts

    def product(u, v):
        return jnp.dot(u, v, preferred_element_type=F32)

    return product(high, b_high) + (product(high, b_low) + product(low, b_high))


def kernel(rec, values, days, counts, prop_in, cov_in, kslab_in, damp, prior, filt_out, smooth_out,
           land, mland, lhs, acc, r1, hs, r2, fh, r3, ri, om, wide, slab, slab_t, brow, maps, brows, kfull, k_t,
           dsrc, dl, psrc, pr, hop_src, hop_in, start_src, start_in, msg, mail, kept, mail_tiles, d_tiles, b_tiles,
           s_rec, r_rec, s_meta, r_meta, s_k, r_k, s_d, r_d, s_p, r_p, s_1, r_1, s_i, r_i, s_2, r_2, s_3, r_3,
           s_a, r_a, s_b, r_b, s_h, r_h, s_s, r_s, s_m, r_m, l_rec, prop, cov, kslab, l_in, meta, plain, s_w, r_w, s_r, pt_parts, c_parts):
    tm, x = lax.axis_index("tm"), lax.axis_index("obs")
    z, y, core = tm // 8, (tm // 2) % 4, tm % 2
    q, xi = x // 2, x % 2
    g, i_row = place_row(y, z)
    e_me = 2 * i_row + q
    c_me = 8 * g + e_me
    j = 2 * xi + core
    lead_tm = lead_of(g)
    is_lead = jnp.logical_and(tm == lead_tm, x == 1)
    sib = tm + 1 - 2 * core
    xp = x + 1 - 2 * xi

    def remote(src, dst, ss, rs, dev):
        return pltpu.make_async_remote_copy(src_ref=src, dst_ref=dst, send_sem=ss, recv_sem=rs, device_id=dev,
                                            device_id_type=MESH)

    drains = []

    def sent(copy, when=None):
        if when is None:
            drains.append(copy.wait_send)
        else:
            drains.append(lambda: pl.when(when)(copy.wait_send))

    barrier = pltpu.get_barrier_semaphore()

    def owner_of(o):
        dq, dy, dz = o // 16, (o // 4) % 4, o % 4
        return ((z + dz) % 4, (y + dy) % 4, (q + dq) % 2, x + dq * (3 - 2 * x)), (
            ((z - dz + 4) % 4) * 8 + ((y - dy + 4) % 4) * 2 + core, x + dq * (3 - 2 * x))

    dr_y, dr_z = row_place(tm // 2)
    d_tm, d_x = dr_z * 8 + dr_y * 2 + x % 2, 2 * (tm % 2) + x // 2
    d_self = jnp.logical_and(d_tm == tm, d_x == x)

    def greet(dev):
        pl.semaphore_signal(barrier, 1, device_id=dev, device_id_type=MESH)

    def greet_source(o, carry):
        greet(owner_of(o)[1])
        return carry

    loads = [pltpu.make_async_copy(a, b, l_in.at[n])
             for n, (a, b) in enumerate(((prop_in, prop), (cov_in, cov), (kslab_in, kslab)))]
    lax.fori_loop(1, 32, greet_source, 0)
    for dev in ((tm, (x + 1) % 4), (tm, (x + 2) % 4), (tm, (x + 3) % 4), (sib, x), (sib, xp),
                (c_me, 2 * xi + core)):
        greet(dev)
    for load in loads:
        load.start()
    slot = lax.broadcasted_iota(jnp.int32, (16, 128), 1)
    part = lax.broadcasted_iota(jnp.int32, (16, 128), 0)
    plain[...] = values[...].astype(F32)

    def mark(c):
        held = jnp.logical_and(jnp.logical_and(slot < counts[c], part % 2 == days[c]), part < 4)
        filled = jnp.where(part < 2, jnp.broadcast_to(plain[pl.ds(c, 1), :], (16, 128)), 1.0)
        return jnp.where(held, filled, 0.0).astype(BF16)

    mland[0] = mark(c_me)
    acc[...] = jnp.zeros_like(acc)
    pl.semaphore_wait(barrier, 37)

    def offset(m):
        return 1 + ((m - 1) * 11 + core * 15) % 31

    def record_copies(m):
        o = offset(m)
        tz, ty, tq, tx = owner_of(o)[0]
        tg, ti = place_row(ty, tz)
        c = 8 * tg + 2 * ti + tq
        dev = (tz * 8 + ty * 2 + core, tx)
        return c, (
            remote(rec.at[pl.ds(pl.multiple_of(c * 128, 128), 128)],
                   land.at[m // 2, pl.ds(pl.multiple_of((m % 2) * 128, 128), 128)], s_rec.at[m], r_rec.at[m], dev),
            remote(meta.at[c], mland.at[m], s_meta.at[m], r_meta.at[m], dev),
        )

    own_rec = pltpu.make_async_copy(rec.at[pl.ds(pl.multiple_of(c_me * 128, 128), 128)],
                                    land.at[0, pl.ds(0, 128)], l_rec)
    own_rec.start()
    def send_record(m, carry):
        c, (a, b) = record_copies(m)
        a.start()
        meta[c] = mark(c)
        b.start()
        return carry

    dsrc[...] = jnp.zeros_like(dsrc)
    dsrc[0:2, :] = damp[...]
    d_copy = remote(dsrc, dl, s_d.at[0], r_d.at[0], (d_tm, d_x))

    @pl.when(d_self)
    def _():
        dl[...] = dsrc[...]

    @pl.when(jnp.logical_not(d_self))
    def _():
        d_copy.start()

    sent(d_copy, jnp.logical_not(d_self))

    lax.fori_loop(1, 32, send_record, 0)
    loads[2].wait()
    def gain_rows(ox, half):
        return pl.ds(pl.multiple_of(ox * 128 + half * 64, 64), 64)

    half_slab = kslab.at[pl.ds(pl.multiple_of(core * 64, 64), 64)]

    def gain_copy(n, ox):
        return remote(half_slab, kfull.at[gain_rows(ox, core)], s_k.at[n], r_k.at[n], (tm, (x + n) % 4))

    def gain_swap(n, half):
        rows = gain_rows((x - n + 4) % 4, half)
        return remote(kfull.at[rows], kfull.at[rows], s_w.at[n], r_w.at[n], (sib, x))

    for n in range(1, 4):
        gain_copy(n, x).start()
        sent(gain_copy(n, x))
    kfull[pl.ds(pl.multiple_of(x * 128, 128), 128), :] = kslab[...]

    def drain_record(m, carry):
        a, b = record_copies(m)[1]
        a.wait_send()
        b.wait_send()
        return carry

    drains.append(lambda: lax.fori_loop(1, 32, drain_record, 0))

    for load in loads[:2]:
        load.wait()
    pt_parts[0], pt_parts[1] = parts_of(prop[...].T)
    c_parts[0], c_parts[1] = parts_of(cov[...])
    own_rec.wait()

    def wait_record(m):
        a, b = record_copies(m)[1]
        b.wait_recv()
        a.wait_recv()

    def gram(p, carry):
        @pl.when(p > 0)
        def _():
            wait_record(2 * p)
        wait_record(2 * p + 1)
        rows = land[p]
        marks = jnp.concatenate([mland[2 * p], mland[2 * p + 1]], axis=1)
        rows_t = rows.T
        lhs[0:512, :] = rows_t * marks[2:3, :]
        lhs[512:1024, :] = rows_t * marks[3:4, :]
        lhs[1024:1040, :] = marks
        acc[...] += jnp.dot(lhs[...], rows, preferred_element_type=F32)
        return carry

    lax.fori_loop(0, 16, gram, 0)

    def first_copies(d, owner):
        return [remote(acc.at[pl.ds(d * 512 + 128 * r, 128), pl.ds(c0, w)], r1.at[d, :, pl.ds(at, w)],
                       s_1.at[2 * d + n], r_1.at[2 * d + n], (sib, x))
                for n, (r, c0, w, at) in enumerate(PARTS[owner])]

    def by_core(step):
        for own in range(2):
            pl.when(core == own)(lambda own=own: step(own))

    peers = ((sib, x), (tm, xp), (sib, xp))
    info_copies = [remote(acc.at[pl.ds(1024, 8), :], ri.at[n], s_i.at[n], r_i.at[n], peers[n]) for n in range(3)]
    def give(own):
        for d in range(2):
            for copy in first_copies(d, 1 - own):
                copy.start()

    def given(own):
        for d in range(2):
            for copy in first_copies(d, 1 - own):
                copy.wait_send()

    by_core(give)
    drains.append(lambda: by_core(given))
    for copy in info_copies:
        copy.start()
        sent(copy)
    second = [remote(hs.at[d], r2.at[d], s_2.at[d], r_2.at[d], (tm, xp)) for d in range(2)]
    third = [remote(fh.at[d], r3.at[d], s_3.at[d], r_3.at[d], (sib, x)) for d in range(2)]
    for d in range(2):
        def add(own, d=d):
            for copy in first_copies(d, own):
                copy.wait_recv()
            for r, c0, w, at in PARTS[own]:
                hs[d, :, at:at + w] = (acc[d * 512 + 128 * r:d * 512 + 128 * r + 128, c0:c0 + w]
                                       + r1[d, :, at:at + w])

        by_core(add)
        second[d].start()
        sent(second[d])
    for copy in info_copies:
        copy.wait_recv()
    info = (acc[1024:1032, :] + ri[0]) + (ri[1] + ri[2])

    @pl.when(jnp.logical_not(d_self))
    def _():
        d_copy.wait_recv()

    d_rows = dl[...]
    for d in range(2):
        keep(d_tiles.at[d], to_tiles(d_rows[d:d + 1, :]))

    wide[0:128, :] = prop[:, pl.ds(pl.multiple_of(j * 128, 128), 128)].T * d_rows[0:1, :]
    wide[128:136, :] = jnp.zeros((8, S), F32)
    for d in range(2):
        second[d].wait_recv()
        fh[d] = hs[d] + r2[d]
        third[d].start()
        sent(third[d])
        def put(own, src, d=d):
            for r, c0, w, at in PARTS[own]:
                om[d, 128 * r:128 * r + 128, c0:c0 + w] = src[d, :, at:at + w]

        by_core(lambda own: put(own, fh))
        third[d].wait_recv()
        by_core(lambda own: put(1 - own, r3))
        for r in range(1, 4):
            for c in range(r):
                om[d, 128 * r:128 * r + 128, 128 * c:128 * c + 128] = (
                    om[d, 128 * c:128 * c + 128, 128 * r:128 * r + 128].T)
        if d == 1:
            wide[...] = dot(wide[...], (pt_parts[0], pt_parts[1])) * d_rows[1:2, :]
        w = wide[...]
        seen = jnp.concatenate([jnp.zeros((128, S), F32), jnp.broadcast_to(info[d:d + 1, :], (8, S))], axis=0)
        wide[...] = w - dot(dot(w, parts_of(om[d])) - seen, (c_parts[0], c_parts[1]))

    lead = (lead_tm, 1)
    by_row = jnp.logical_and(xi == 0, (1 - q) * (i_row + 1) // 2 % 2 + q * i_row // 3 == 1)
    to_lead = (lead_tm + jnp.where(by_row, core, 0), jnp.where(by_row, x, 1))
    slab_cols = pl.multiple_of(j * 128, 128)
    even_copy = remote(slab_t, maps.at[e_me, :, pl.ds(slab_cols, 128)], s_a.at[0], r_a.at[e_me * 4 + j], to_lead)
    odd_copy = remote(slab, maps.at[e_me, pl.ds(slab_cols, 128), :], s_a.at[0], r_a.at[e_me * 4 + j], to_lead)
    b_copy = remote(brow, brows.at[e_me], s_b.at[0], r_b.at[e_me], lead)

    @pl.when(q == 0)
    def _():
        slab_t[...] = wide[0:128, :].T

    @pl.when(q == 1)
    def _():
        slab[...] = wide[0:128, :]

    @pl.when(is_lead)
    def _():
        maps[0, :, 256:384] = slab_t[...]

    even_send = jnp.logical_and(q == 0, jnp.logical_not(is_lead))

    @pl.when(even_send)
    def _():
        even_copy.start()

    sent(even_copy, even_send)

    @pl.when(q == 1)
    def _():
        odd_copy.start()

    sent(odd_copy, q == 1)

    brow[...] = wide[128:136, :]

    @pl.when(j == 0)
    def _():
        b_copy.start()

    sent(b_copy, j == 0)

    psrc[...] = jnp.broadcast_to(prior[...], (8, 128))
    p_copy = remote(psrc, pr.at[x], s_p.at[0], r_p.at[x], (lead_of(0), 1))
    p_send = jnp.logical_and(tm == lead_of(0), x != 1)

    @pl.when(p_send)
    def _():
        p_copy.start()

    sent(p_copy, p_send)

    @pl.when(jnp.logical_and(tm == lead_of(0), x == 1))
    def _():
        pr[1] = psrc[...]

    def pass_on(e):
        if e % 2 == 0:
            place = maps.at[e, :, pl.ds(slab_cols, 128)]
        else:
            place = maps.at[e, pl.ds(slab_cols, 128), :]
        return remote(place, place, s_r.at[e], r_a.at[e * 4 + j], lead)

    in_middle = jnp.logical_and(i_row == 0, xi == 0)
    for at_q, passed in ((0, (2, 4)), (1, (7,))):
        relays = jnp.logical_and(in_middle, q == at_q)

        @pl.when(relays)
        def _(passed=passed):
            for e in passed:
                pass_on(e).wait_recv()
                pass_on(e).start()

        for e in passed:
            sent(pass_on(e), relays)

    for n in range(1, 4):
        gain_copy(n, (x - n + 4) % 4).wait_recv()
        gain_swap(n, core).start()
        sent(gain_swap(n, core))
    for n in range(1, 4):
        gain_swap(n, 1 - core).wait_recv()
    k_t[...] = kfull[...].T

    to_self = j == x

    def wait_mail(c):
        @pl.when(jnp.logical_not(jnp.logical_and(to_self, c == c_me)))
        def _():
            remote(msg, mail.at[c], s_m.at[0], r_m.at[c], (sib, x)).wait_recv()

    def expand(c, carry):
        wait_mail(c)
        keep(mail_tiles.at[c, 0], to_tiles(mail[c, 5:6, :]))
        keep(mail_tiles.at[c, 1], to_tiles(mail[c, 2:3, :]))
        return carry

    early_end = jnp.maximum(tm, 8 * (g - 1))
    early_lead = jnp.maximum(tm, 8 * (g - 2))

    next_g = (g + 1) % 4
    hop_copy = remote(hop_src, hop_in, s_h.at[0], r_h.at[0], (lead_of(next_g), 1))

    def start_copy(e, n):
        sy, sz = row_place(4 * g + e // 2)
        return remote(start_src.at[e], start_in, s_s.at[e * 4 + n], r_s.at[0],
                      (sz * 8 + sy * 2 + n % 2, 2 * (e % 2) + n // 2))

    @pl.when(is_lead)
    def _():
        @pl.when(g == 0)
        def _():
            for ox in (0, 2, 3):
                remote(psrc, pr.at[ox], s_p.at[0], r_p.at[ox], (sib, x)).wait_recv()
            for ox in range(4):
                hop_in[:, 128 * ox:128 * ox + 128] = pr[ox]

        for e in range(8):
            for n in range(4):
                if (e, n) == (0, 2):
                    continue
                if e % 2 == 0:
                    remote(slab_t, maps.at[e, :, pl.ds(128 * n, 128)], s_a.at[0], r_a.at[e * 4 + n],
                           (sib, x)).wait_recv()
                else:
                    remote(slab, maps.at[e, pl.ds(128 * n, 128), :], s_a.at[0], r_a.at[e * 4 + n],
                           (sib, x)).wait_recv()
            remote(brow, brows.at[e], s_b.at[0], r_b.at[e], (sib, x)).wait_recv()

        for e in range(0, 8, 2):
            keep(b_tiles.at[e // 2], to_tiles(brows[e, 0:1, :]))

        lax.fori_loop(tm, early_lead, expand, 0)

        @pl.when(g > 0)
        def _():
            hop_copy.wait_recv()

        row = hop_in[0:1, :]
        for e in range(0, 8, 2):
            start_src[e] = jnp.broadcast_to(row, (8, S))
            tiles = row_times(maps.at[e], row)
            tiles = [tiles[k] + kept_tile(b_tiles.at[e // 2], k) for k in range(64)]
            keep(b_tiles.at[e // 2], tiles)
            row = col_times(maps.at[e + 1], tiles) + brows[e + 1, 0:1, :]
        hop_src[...] = jnp.broadcast_to(row, (8, S))

        @pl.when(g < 3)
        def _():
            hop_copy.start()

        for e in range(7, 0, -2):
            start_src[e] = jnp.broadcast_to(
                to_row([kept_tile(b_tiles.at[e // 2], k) for k in range(64)]), (8, S))
        start_in[...] = start_src[0]
        for e in range(7, -1, -1):
            for n in range(4):
                if (e, n) != (0, 2):
                    start_copy(e, n).start()

    def drain_leader():
        for e in range(8):
            for n in range(4):
                if (e, n) != (0, 2):
                    start_copy(e, n).wait_send()

        @pl.when(g < 3)
        def _():
            hop_copy.wait_send()

    drains.append(lambda: pl.when(is_lead)(drain_leader))

    lax.fori_loop(jnp.where(is_lead, early_lead, tm), early_end, expand, 0)

    @pl.when(jnp.logical_not(is_lead))
    def _():
        start_copy(0, 0).wait_recv()

    before = start_in[0:1, :]

    def day(d, ahead):
        moved = [kept_tile(d_tiles.at[d], k) * ahead[k] for k in range(64)]
        back = row_times(cov, col_times(om.at[d], moved) - info[d:d + 1, :])
        return to_row([moved[k] - back[k] for k in range(64)])

    first = day(0, row_times(prop, before))
    ahead = row_times(prop, first)
    last = day(1, ahead)
    d_first, d_last = d_rows[0:1, :], d_rows[1:2, :]
    msg[0:1, :] = first
    msg[1:2, :] = last
    msg[2:3, :] = d_last * (last - d_last * to_row(ahead))
    msg[3:4, :] = to_row(row_times(prop, last))
    msg[4:5, :] = d_first
    msg[5:6, :] = d_last
    msg[6:8, :] = jnp.zeros((2, S), F32)

    def mail_copy(n):
        return remote(msg, mail.at[c_me], s_m.at[n], r_m.at[c_me], (n, j))

    @pl.when(to_self)
    def _():
        mail[c_me] = msg[...]

    def to_other(n):
        return jnp.logical_or(n != tm, jnp.logical_not(to_self))

    def post(n, carry):
        @pl.when(to_other(n))
        def _():
            mail_copy(n).start()
        return carry

    lax.fori_loop(0, 32, post, 0)

    def drain_post(n, carry):
        @pl.when(to_other(n))
        def _():
            mail_copy(n).wait_send()
        return carry

    drains.append(lambda: lax.fori_loop(0, 32, drain_post, 0))

    own_cols = pl.ds(pl.multiple_of(x * 128, 128), 128)

    lax.fori_loop(early_end, 32, expand, 0)

    def back(c, state, damp_next):
        gap = damp_next * (state - damp_next * mail[c, 3:4, :])
        later = row_times(kfull, gap)
        scale, shift = mail_tiles.at[c, 0], mail_tiles.at[c, 1]
        gaps = [kept_tile(scale, k) * later[k] + kept_tile(shift, k) for k in range(64)]
        return mail[c, 0:1, :] + col_times(k_t, gaps), later

    def back_step(n, carry):
        state, damp_next = carry
        c = 31 - n
        return back(c, state, damp_next)[0], mail[c, 4:5, :]

    zero = jnp.zeros((1, S), F32)
    state, damp_next = lax.fori_loop(0, 31 - tm, back_step, (zero, zero))
    state, later = back(tm, state, damp_next)
    kept[0:1, :] = state
    kept[1:2, :] = mail[tm, 1:2, :] + to_row(later)
    smooth_out[...] = kept[0:2, own_cols]
    filt_out[...] = mail[tm, 0:2, own_cols]

    def drain_mail(n, carry):
        wait_mail(n)
        return carry

    lax.fori_loop(0, tm, drain_mail, 0)
    for drain in drains:
        drain()


def hand_out(filt, smooth, filt_out, smooth_out):
    filt_out[...] = filt[...]
    smooth_out[...] = smooth[...]


def local(records, obs_values, block_day, block_count, propagator_matrix, analysis_cov, unattenuated_multiplier,
          damping, prior_mean):
    vmem = pl.BlockSpec(memory_space=pltpu.VMEM)
    hbm = pl.BlockSpec(memory_space=pl.ANY)
    smem = pl.BlockSpec(memory_space=pltpu.SMEM)
    dma = pltpu.SemaphoreType.DMA
    results = pl.pallas_call(
        kernel,
        out_shape=(jax.ShapeDtypeStruct((2, 128), F32), jax.ShapeDtypeStruct((2, 128), F32)),
        in_specs=[hbm, vmem, smem, smem] + [hbm] * 3 + [vmem] * 2,
        out_specs=(vmem, vmem),
        scratch_shapes=[
            pltpu.VMEM((16, 256, S), BF16),
            pltpu.VMEM((32, 16, 128), BF16),
            pltpu.VMEM((1040, 256), BF16),
            pltpu.VMEM((1040, S), F32),
            pltpu.VMEM((2, 128, 640), F32),
            pltpu.VMEM((2, 128, 640), F32),
            pltpu.VMEM((2, 128, 640), F32),
            pltpu.VMEM((2, 128, 640), F32),
            pltpu.VMEM((2, 128, 640), F32),
            pltpu.VMEM((3, 8, S), F32),
            pltpu.VMEM((2, S, S), F32),
            pltpu.VMEM((136, S), F32),
            pltpu.VMEM((128, S), F32),
            pltpu.VMEM((S, 128), F32),
            pltpu.VMEM((8, S), F32),
            pltpu.VMEM((8, S, S), F32),
            pltpu.VMEM((8, 8, S), F32),
            pltpu.VMEM((S, S), F32),
            pltpu.VMEM((S, S), F32),
            pltpu.VMEM((8, S), F32),
            pltpu.VMEM((8, S), F32),
            pltpu.VMEM((8, 128), F32),
            pltpu.VMEM((4, 8, 128), F32),
            pltpu.VMEM((8, S), F32),
            pltpu.VMEM((8, S), F32),
            pltpu.VMEM((8, 8, S), F32),
            pltpu.VMEM((8, S), F32),
            pltpu.VMEM((8, S), F32),
            pltpu.VMEM((32, 8, S), F32),
            pltpu.VMEM((8, S), F32),
            pltpu.VMEM((32, 2, S, 128), F32),
            pltpu.VMEM((2, S, 128), F32),
            pltpu.VMEM((4, S, 128), F32),
            dma((32,)), dma((32,)), dma((32,)), dma((32,)),
            dma((4,)), dma((4,)), dma((1,)), dma((1,)), dma((1,)), dma((4,)),
            dma((4,)), dma((4,)), dma((3,)), dma((3,)), dma((2,)), dma((2,)), dma((2,)), dma((2,)),
            dma((1,)), dma((32,)), dma((1,)), dma((8,)), dma((1,)), dma((1,)),
            dma((32,)), dma((1,)), dma((32,)), dma((32,)), dma,
            pltpu.VMEM((S, S), F32), pltpu.VMEM((S, S), F32), pltpu.VMEM((128, S), F32), dma((3,)),
            pltpu.VMEM((32, 16, 128), BF16),
            pltpu.VMEM((32, 128), F32),
            dma((4,)), dma((4,)), dma((8,)),
            pltpu.VMEM((2, S, S), BF16), pltpu.VMEM((2, S, S), BF16),
        ],
        compiler_params=pltpu.CompilerParams(collective_id=0, has_side_effects=True, vmem_limit_bytes=56 << 20),
        cost_estimate=pl.CostEstimate(flops=10**10, bytes_accessed=10**8, transcendentals=0),
    )(records, obs_values.reshape(32, 128), block_day, block_count, propagator_matrix, analysis_cov, unattenuated_multiplier, damping, prior_mean.reshape(1, 128))
    return pl.pallas_call(
        hand_out,
        out_shape=(jax.ShapeDtypeStruct((2, 128), F32), jax.ShapeDtypeStruct((2, 128), F32)),
        in_specs=[vmem, vmem],
        out_specs=(vmem, vmem),
    )(*results)


def solution(mesh):
    return jax.shard_map(
        local,
        mesh=mesh,
        in_specs=(
            P(("tm", "obs"), None),
            P(("tm", "obs")),
            P(("tm", "obs")),
            P(("tm", "obs")),
            P(),
            P(),
            P("obs", None),
            P("tm", None),
            P("obs"),
        ),
        out_specs=(P("tm", "obs"), P("tm", "obs")),
        check_vma=False,
    )
```

```python
import jax
import jax.numpy as jnp
from jax import lax
from jax.experimental import pallas as pl
from jax.experimental.pallas import tpu as pltpu
from jax.sharding import PartitionSpec as P

MESH = pl.DeviceIdType.MESH
F32 = jnp.float32
BF16 = jnp.bfloat16
S = 512


def row_place(r):
    g, i = r // 4, r % 4
    im = i % 3
    return (2 * (g // 2) + im * (im + 1) // 2) % 4, g + (i // 3) * (3 - 2 * g)


def place_row(y, z):
    odd = y % 2
    extra = (1 - odd) * ((y // 2 + z // 2) % 2)
    g = z + extra * (3 - 2 * z)
    return g, odd * (1 + ((y - 2 * (z // 2) + 4) % 4) // 2) + 3 * extra


def lead_of(g):
    return g * 8 + g // 2 * 4


PARTS = (((0, 0, 512, 0), (3, 384, 128, 512)), ((1, 128, 384, 0), (2, 384, 128, 384), (2, 256, 128, 512)))


def row_times(ref, row):
    wide = jnp.broadcast_to(row, (8, S))
    tiles = []
    for k in range(0, S, 8):
        t = [ref[k:k + 8, n:n + 128] * wide[:, n:n + 128] for n in range(0, S, 128)]
        tiles.append(jnp.broadcast_to(jnp.sum((t[0] + t[1]) + (t[2] + t[3]), axis=1, keepdims=True), (8, 128)))
    return tiles


def col_times(ref, tiles):
    out = []
    for n in range(0, S, 128):
        total = [None] * 4
        for k in range(64):
            p = ref[8 * k:8 * k + 8, n:n + 128] * tiles[k]
            total[k % 4] = p if total[k % 4] is None else total[k % 4] + p
        out.append(jnp.sum((total[0] + total[1]) + (total[2] + total[3]), axis=0, keepdims=True))
    return jnp.concatenate(out, axis=1)


def diagonals():
    lead = lax.broadcasted_iota(jnp.int32, (8, 128), 1) - lax.broadcasted_iota(jnp.int32, (8, 128), 0)
    return [lead == 8 * k for k in range(16)]


def to_row(tiles):
    marks = diagonals()
    out = []
    for n in range(4):
        picked = [jnp.where(marks[k], tiles[16 * n + k], 0.0) for k in range(16)]
        while len(picked) > 1:
            picked = [picked[k] + picked[k + 1] for k in range(0, len(picked), 2)]
        out.append(jnp.sum(picked[0], axis=0, keepdims=True))
    return jnp.concatenate(out, axis=1)


def to_tiles(row):
    marks = diagonals()
    tiles = []
    for n in range(4):
        part = jnp.broadcast_to(row[:, 128 * n:128 * n + 128], (8, 128))
        for k in range(16):
            tiles.append(jnp.broadcast_to(
                jnp.sum(jnp.where(marks[k], part, 0.0), axis=1, keepdims=True), (8, 128)))
    return tiles


def keep(ref, tiles):
    for k in range(64):
        ref[8 * k:8 * k + 8, :] = tiles[k]


def kept_tile(ref, k):
    return ref[8 * k:8 * k + 8, :]


def parts_of(a):
    high = a.astype(BF16)
    return high, (a - high.astype(F32)).astype(BF16)


def dot(a, parts):
    high, low = parts_of(a)
    b_high, b_low = parts

    def product(u, v):
        return jnp.dot(u, v, preferred_element_type=F32)

    return product(high, b_high) + (product(high, b_low) + product(low, b_high))


def kernel(rec, values, days, counts, prop_in, cov_in, kslab_in, damp, prior, filt_out, smooth_out,
           land, mland, lhs, acc, r1, hs, r2, fh, r3, ri, om, wide, slab, slab_t, brow, maps, brows, kfull, k_t,
           dsrc, dl, psrc, pr, hop_src, hop_in, start_src, start_in, msg, mail, kept, mail_tiles, d_tiles, b_tiles,
           s_rec, r_rec, s_meta, r_meta, s_k, r_k, s_d, r_d, s_p, r_p, s_1, r_1, s_i, r_i, s_2, r_2, s_3, r_3,
           s_a, r_a, s_b, r_b, s_h, r_h, s_s, r_s, s_m, r_m, l_rec, prop, cov, kslab, l_in, meta, plain, s_w, r_w, s_r, pt_parts, c_parts):
    tm, x = lax.axis_index("tm"), lax.axis_index("obs")
    z, y, core = tm // 8, (tm // 2) % 4, tm % 2
    q, xi = x // 2, x % 2
    g, i_row = place_row(y, z)
    e_me = 2 * i_row + q
    c_me = 8 * g + e_me
    j = 2 * xi + core
    lead_tm = lead_of(g)
    is_lead = jnp.logical_and(tm == lead_tm, x == 1)
    sib = tm + 1 - 2 * core
    xp = x + 1 - 2 * xi

    def remote(src, dst, ss, rs, dev):
        return pltpu.make_async_remote_copy(src_ref=src, dst_ref=dst, send_sem=ss, recv_sem=rs, device_id=dev,
                                            device_id_type=MESH)

    drains = []

    def sent(copy, when=None):
        if when is None:
            drains.append(copy.wait_send)
        else:
            drains.append(lambda: pl.when(when)(copy.wait_send))

    barrier = pltpu.get_barrier_semaphore()

    def owner_of(o):
        dq, dy, dz = o // 16, (o // 4) % 4, o % 4
        return ((z + dz) % 4, (y + dy) % 4, (q + dq) % 2, x + dq * (3 - 2 * x)), (
            ((z - dz + 4) % 4) * 8 + ((y - dy + 4) % 4) * 2 + core, x + dq * (3 - 2 * x))

    dr_y, dr_z = row_place(tm // 2)
    d_tm, d_x = dr_z * 8 + dr_y * 2 + x % 2, 2 * (tm % 2) + x // 2
    d_self = jnp.logical_and(d_tm == tm, d_x == x)

    def greet(dev):
        pl.semaphore_signal(barrier, 1, device_id=dev, device_id_type=MESH)

    def greet_source(o, carry):
        greet(owner_of(o)[1])
        return carry

    loads = [pltpu.make_async_copy(a, b, l_in.at[n])
             for n, (a, b) in enumerate(((prop_in, prop), (cov_in, cov), (kslab_in, kslab)))]
    lax.fori_loop(1, 32, greet_source, 0)
    for dev in ((tm, (x + 1) % 4), (tm, (x + 2) % 4), (tm, (x + 3) % 4), (sib, x), (sib, xp),
                (c_me, 2 * xi + core)):
        greet(dev)
    for load in loads:
        load.start()
    slot = lax.broadcasted_iota(jnp.int32, (16, 128), 1)
    part = lax.broadcasted_iota(jnp.int32, (16, 128), 0)
    plain[...] = values[...].astype(F32)

    def mark(c):
        held = jnp.logical_and(jnp.logical_and(slot < counts[c], part % 2 == days[c]), part < 4)
        filled = jnp.where(part < 2, jnp.broadcast_to(plain[pl.ds(c, 1), :], (16, 128)), 1.0)
        return jnp.where(held, filled, 0.0).astype(BF16)

    mland[0] = mark(c_me)
    acc[...] = jnp.zeros_like(acc)
    pl.semaphore_wait(barrier, 37)

    def offset(m):
        return 1 + ((m - 1) * 11 + core * 15) % 31

    def record_copies(m):
        o = offset(m)
        tz, ty, tq, tx = owner_of(o)[0]
        tg, ti = place_row(ty, tz)
        c = 8 * tg + 2 * ti + tq
        dev = (tz * 8 + ty * 2 + core, tx)
        return c, (
            remote(rec.at[pl.ds(pl.multiple_of(c * 128, 128), 128)],
                   land.at[m // 2, pl.ds(pl.multiple_of((m % 2) * 128, 128), 128)], s_rec.at[m], r_rec.at[m], dev),
            remote(meta.at[c], mland.at[m], s_meta.at[m], r_meta.at[m], dev),
        )

    own_rec = pltpu.make_async_copy(rec.at[pl.ds(pl.multiple_of(c_me * 128, 128), 128)],
                                    land.at[0, pl.ds(0, 128)], l_rec)
    own_rec.start()
    def send_record(m, carry):
        c, (a, b) = record_copies(m)
        a.start()
        meta[c] = mark(c)
        b.start()
        return carry

    dsrc[...] = jnp.zeros_like(dsrc)
    dsrc[0:2, :] = damp[...]
    d_copy = remote(dsrc, dl, s_d.at[0], r_d.at[0], (d_tm, d_x))

    @pl.when(d_self)
    def _():
        dl[...] = dsrc[...]

    @pl.when(jnp.logical_not(d_self))
    def _():
        d_copy.start()

    sent(d_copy, jnp.logical_not(d_self))

    lax.fori_loop(1, 32, send_record, 0)
    loads[2].wait()
    def gain_rows(ox, half):
        return pl.ds(pl.multiple_of(ox * 128 + half * 64, 64), 64)

    half_slab = kslab.at[pl.ds(pl.multiple_of(core * 64, 64), 64)]

    def gain_copy(n, ox):
        return remote(half_slab, kfull.at[gain_rows(ox, core)], s_k.at[n], r_k.at[n], (tm, (x + n) % 4))

    def gain_swap(n, half):
        rows = gain_rows((x - n + 4) % 4, half)
        return remote(kfull.at[rows], kfull.at[rows], s_w.at[n], r_w.at[n], (sib, x))

    for n in range(1, 4):
        gain_copy(n, x).start()
        sent(gain_copy(n, x))
    kfull[pl.ds(pl.multiple_of(x * 128, 128), 128), :] = kslab[...]

    def drain_record(m, carry):
        a, b = record_copies(m)[1]
        a.wait_send()
        b.wait_send()
        return carry

    drains.append(lambda: lax.fori_loop(1, 32, drain_record, 0))

    for load in loads[:2]:
        load.wait()
    pt_parts[0], pt_parts[1] = parts_of(prop[...].T)
    c_parts[0], c_parts[1] = parts_of(cov[...])
    own_rec.wait()

    def wait_record(m):
        a, b = record_copies(m)[1]
        b.wait_recv()
        a.wait_recv()

    def gram(p, carry):
        @pl.when(p > 0)
        def _():
            wait_record(2 * p)
        wait_record(2 * p + 1)
        rows = land[p]
        marks = jnp.concatenate([mland[2 * p], mland[2 * p + 1]], axis=1)
        rows_t = rows.T
        lhs[0:512, :] = rows_t * marks[2:3, :]
        lhs[512:1024, :] = rows_t * marks[3:4, :]
        lhs[1024:1040, :] = marks
        acc[...] += jnp.dot(lhs[...], rows, preferred_element_type=F32)
        return carry

    lax.fori_loop(0, 16, gram, 0)

    def first_copies(d, owner):
        return [remote(acc.at[pl.ds(d * 512 + 128 * r, 128), pl.ds(c0, w)], r1.at[d, :, pl.ds(at, w)],
                       s_1.at[3 * d + n], r_1.at[3 * d + n], (sib, x))
                for n, (r, c0, w, at) in enumerate(PARTS[owner])]

    def by_core(step):
        for own in range(2):
            pl.when(core == own)(lambda own=own: step(own))

    peers = ((sib, x), (tm, xp), (sib, xp))
    info_copies = [remote(acc.at[pl.ds(1024, 8), :], ri.at[n], s_i.at[n], r_i.at[n], peers[n]) for n in range(3)]
    def give(own):
        for d in range(2):
            for copy in first_copies(d, 1 - own):
                copy.start()

    def given(own):
        for d in range(2):
            for copy in first_copies(d, 1 - own):
                copy.wait_send()

    by_core(give)
    drains.append(lambda: by_core(given))
    for copy in info_copies:
        copy.start()
        sent(copy)
    def pieces(src, dst, ss, rs, dev):
        return [[remote(src.at[d, :, pl.ds(0, 512)], dst.at[d, :, pl.ds(0, 512)], ss.at[2 * d], rs.at[2 * d], dev),
                 remote(src.at[d, pl.ds(0, 64), pl.ds(512, 128)], dst.at[d, pl.ds(0, 64), pl.ds(512, 128)],
                        ss.at[2 * d + 1], rs.at[2 * d + 1], dev)] for d in range(2)]

    second = pieces(hs, r2, s_2, r_2, (tm, xp))
    third = pieces(fh, r3, s_3, r_3, (sib, x))
    left = lax.broadcasted_iota(jnp.int32, (64, 128), 1) < 64
    corner = jnp.logical_and(lax.broadcasted_iota(jnp.int32, (128, 128), 1) < 64,
                             lax.broadcasted_iota(jnp.int32, (128, 128), 0) >= 64)

    for d in range(2):
        def add(own, d=d):
            for copy in first_copies(d, own):
                copy.wait_recv()
            for r, c0, w, at in PARTS[own]:
                hs[d, :, at:at + w] = (acc[d * 512 + 128 * r:d * 512 + 128 * r + 128, c0:c0 + w]
                                       + r1[d, :, at:at + w])

        by_core(add)
        hs[d, 64:128, 0:128] = jnp.where(left, pltpu.roll(hs[d, 64:128, 512:640], 64, 1), hs[d, 64:128, 0:128])
        for copy in second[d]:
            copy.start()
            sent(copy)
    for copy in info_copies:
        copy.wait_recv()
    info = (acc[1024:1032, :] + ri[0]) + (ri[1] + ri[2])

    @pl.when(jnp.logical_not(d_self))
    def _():
        d_copy.wait_recv()

    d_rows = dl[...]
    for d in range(2):
        keep(d_tiles.at[d], to_tiles(d_rows[d:d + 1, :]))

    wide[0:128, :] = prop[:, pl.ds(pl.multiple_of(j * 128, 128), 128)].T * d_rows[0:1, :]
    wide[128:136, :] = jnp.zeros((8, S), F32)
    for d in range(2):
        for copy in second[d]:
            copy.wait_recv()
        fh[d, :, 0:512] = hs[d, :, 0:512] + r2[d, :, 0:512]
        fh[d, 0:64, 512:640] = hs[d, 0:64, 512:640] + r2[d, 0:64, 512:640]
        for copy in third[d]:
            copy.start()
            sent(copy)
        def put(own, src, d=d):
            for r, c0, w, at in PARTS[own]:
                if at < 512:
                    om[d, 128 * r:128 * r + 128, c0:c0 + w] = src[d, :, at:at + w]
                else:
                    om[d, 128 * r:128 * r + 64, c0:c0 + w] = src[d, 0:64, at:at + w]
                    om[d, 128 * r + 64:128 * r + 128, c0:c0 + w] = pltpu.roll(src[d, 64:128, 0:128], 64, 1)

        by_core(lambda own: put(own, fh))
        for copy in third[d]:
            copy.wait_recv()
        by_core(lambda own: put(1 - own, r3))
        for r in range(4):
            whole = om[d, 128 * r:128 * r + 128, 128 * r:128 * r + 128]
            om[d, 128 * r:128 * r + 128, 128 * r:128 * r + 128] = jnp.where(corner, whole.T, whole)
            for c in range(r):
                om[d, 128 * r:128 * r + 128, 128 * c:128 * c + 128] = (
                    om[d, 128 * c:128 * c + 128, 128 * r:128 * r + 128].T)
        if d == 1:
            wide[...] = dot(wide[...], (pt_parts[0], pt_parts[1])) * d_rows[1:2, :]
        w = wide[...]
        seen = jnp.concatenate([jnp.zeros((128, S), F32), jnp.broadcast_to(info[d:d + 1, :], (8, S))], axis=0)
        wide[...] = w - dot(dot(w, parts_of(om[d])) - seen, (c_parts[0], c_parts[1]))

    lead = (lead_tm, 1)
    by_row = jnp.logical_and(xi == 0, (1 - q) * (i_row + 1) // 2 % 2 + q * i_row // 3 == 1)
    to_lead = (lead_tm + jnp.where(by_row, core, 0), jnp.where(by_row, x, 1))
    slab_cols = pl.multiple_of(j * 128, 128)
    even_copy = remote(slab_t, maps.at[e_me, :, pl.ds(slab_cols, 128)], s_a.at[0], r_a.at[e_me * 4 + j], to_lead)
    odd_copy = remote(slab, maps.at[e_me, pl.ds(slab_cols, 128), :], s_a.at[0], r_a.at[e_me * 4 + j], to_lead)
    b_copy = remote(brow, brows.at[e_me], s_b.at[0], r_b.at[e_me], lead)

    @pl.when(q == 0)
    def _():
        slab_t[...] = wide[0:128, :].T

    @pl.when(q == 1)
    def _():
        slab[...] = wide[0:128, :]

    @pl.when(is_lead)
    def _():
        maps[0, :, 256:384] = slab_t[...]

    even_send = jnp.logical_and(q == 0, jnp.logical_not(is_lead))

    @pl.when(even_send)
    def _():
        even_copy.start()

    sent(even_copy, even_send)

    @pl.when(q == 1)
    def _():
        odd_copy.start()

    sent(odd_copy, q == 1)

    brow[...] = wide[128:136, :]

    @pl.when(j == 0)
    def _():
        b_copy.start()

    sent(b_copy, j == 0)

    psrc[...] = jnp.broadcast_to(prior[...], (8, 128))
    p_copy = remote(psrc, pr.at[x], s_p.at[0], r_p.at[x], (lead_of(0), 1))
    p_send = jnp.logical_and(tm == lead_of(0), x != 1)

    @pl.when(p_send)
    def _():
        p_copy.start()

    sent(p_copy, p_send)

    @pl.when(jnp.logical_and(tm == lead_of(0), x == 1))
    def _():
        pr[1] = psrc[...]

    def pass_on(e):
        if e % 2 == 0:
            place = maps.at[e, :, pl.ds(slab_cols, 128)]
        else:
            place = maps.at[e, pl.ds(slab_cols, 128), :]
        return remote(place, place, s_r.at[e], r_a.at[e * 4 + j], lead)

    in_middle = jnp.logical_and(i_row == 0, xi == 0)
    for at_q, passed in ((0, (2, 4)), (1, (7,))):
        relays = jnp.logical_and(in_middle, q == at_q)

        @pl.when(relays)
        def _(passed=passed):
            for e in passed:
                pass_on(e).wait_recv()
                pass_on(e).start()

        for e in passed:
            sent(pass_on(e), relays)

    for n in range(1, 4):
        gain_copy(n, (x - n + 4) % 4).wait_recv()
        gain_swap(n, core).start()
        sent(gain_swap(n, core))
    for n in range(1, 4):
        gain_swap(n, 1 - core).wait_recv()
    k_t[...] = kfull[...].T

    to_self = j == x

    def wait_mail(c):
        @pl.when(jnp.logical_not(jnp.logical_and(to_self, c == c_me)))
        def _():
            remote(msg, mail.at[c], s_m.at[0], r_m.at[c], (sib, x)).wait_recv()

    def expand(c, carry):
        wait_mail(c)
        keep(mail_tiles.at[c, 0], to_tiles(mail[c, 5:6, :]))
        keep(mail_tiles.at[c, 1], to_tiles(mail[c, 2:3, :]))
        return carry

    early_end = jnp.maximum(tm, 8 * (g - 1))
    early_lead = jnp.maximum(tm, 8 * (g - 2))

    next_g = (g + 1) % 4
    hop_copy = remote(hop_src, hop_in, s_h.at[0], r_h.at[0], (lead_of(next_g), 1))

    def start_copy(e, n):
        sy, sz = row_place(4 * g + e // 2)
        return remote(start_src.at[e], start_in, s_s.at[e * 4 + n], r_s.at[0],
                      (sz * 8 + sy * 2 + n % 2, 2 * (e % 2) + n // 2))

    @pl.when(is_lead)
    def _():
        @pl.when(g == 0)
        def _():
            for ox in (0, 2, 3):
                remote(psrc, pr.at[ox], s_p.at[0], r_p.at[ox], (sib, x)).wait_recv()
            for ox in range(4):
                hop_in[:, 128 * ox:128 * ox + 128] = pr[ox]

        for e in range(8):
            for n in range(4):
                if (e, n) == (0, 2):
                    continue
                if e % 2 == 0:
                    remote(slab_t, maps.at[e, :, pl.ds(128 * n, 128)], s_a.at[0], r_a.at[e * 4 + n],
                           (sib, x)).wait_recv()
                else:
                    remote(slab, maps.at[e, pl.ds(128 * n, 128), :], s_a.at[0], r_a.at[e * 4 + n],
                           (sib, x)).wait_recv()
            remote(brow, brows.at[e], s_b.at[0], r_b.at[e], (sib, x)).wait_recv()

        for e in range(0, 8, 2):
            keep(b_tiles.at[e // 2], to_tiles(brows[e, 0:1, :]))

        lax.fori_loop(tm, early_lead, expand, 0)

        @pl.when(g > 0)
        def _():
            hop_copy.wait_recv()

        row = hop_in[0:1, :]
        for e in range(0, 8, 2):
            start_src[e] = jnp.broadcast_to(row, (8, S))
            tiles = row_times(maps.at[e], row)
            tiles = [tiles[k] + kept_tile(b_tiles.at[e // 2], k) for k in range(64)]
            row = col_times(maps.at[e + 1], tiles) + brows[e + 1, 0:1, :]
            start_src[e + 1] = jnp.broadcast_to(to_row(tiles), (8, S))
        hop_src[...] = jnp.broadcast_to(row, (8, S))

        @pl.when(g < 3)
        def _():
            hop_copy.start()

        start_in[...] = start_src[0]
        for e in range(7, -1, -1):
            for n in range(4):
                if (e, n) != (0, 2):
                    start_copy(e, n).start()

    def drain_leader():
        for e in range(8):
            for n in range(4):
                if (e, n) != (0, 2):
                    start_copy(e, n).wait_send()

        @pl.when(g < 3)
        def _():
            hop_copy.wait_send()

    drains.append(lambda: pl.when(is_lead)(drain_leader))

    lax.fori_loop(jnp.where(is_lead, early_lead, tm), early_end, expand, 0)

    @pl.when(jnp.logical_not(is_lead))
    def _():
        start_copy(0, 0).wait_recv()

    before = start_in[0:1, :]

    def day(d, ahead):
        moved = [kept_tile(d_tiles.at[d], k) * ahead[k] for k in range(64)]
        back = row_times(cov, col_times(om.at[d], moved) - info[d:d + 1, :])
        return to_row([moved[k] - back[k] for k in range(64)])

    first = day(0, row_times(prop, before))
    ahead = row_times(prop, first)
    last = day(1, ahead)
    d_first, d_last = d_rows[0:1, :], d_rows[1:2, :]
    msg[0:1, :] = first
    msg[1:2, :] = last
    msg[2:3, :] = d_last * (last - d_last * to_row(ahead))
    msg[3:4, :] = to_row(row_times(prop, last))
    msg[4:5, :] = d_first
    msg[5:6, :] = d_last
    msg[6:8, :] = jnp.zeros((2, S), F32)

    def mail_copy(n):
        return remote(msg, mail.at[c_me], s_m.at[n], r_m.at[c_me], (n, j))

    @pl.when(to_self)
    def _():
        mail[c_me] = msg[...]

    def to_other(n):
        return jnp.logical_or(n != tm, jnp.logical_not(to_self))

    def post(n, carry):
        @pl.when(to_other(n))
        def _():
            mail_copy(n).start()
        return carry

    lax.fori_loop(0, 32, post, 0)

    def drain_post(n, carry):
        @pl.when(to_other(n))
        def _():
            mail_copy(n).wait_send()
        return carry

    drains.append(lambda: lax.fori_loop(0, 32, drain_post, 0))

    own_cols = pl.ds(pl.multiple_of(x * 128, 128), 128)

    lax.fori_loop(early_end, 32, expand, 0)

    def back(c, state, damp_next):
        gap = damp_next * (state - damp_next * mail[c, 3:4, :])
        later = row_times(kfull, gap)
        scale, shift = mail_tiles.at[c, 0], mail_tiles.at[c, 1]
        gaps = [kept_tile(scale, k) * later[k] + kept_tile(shift, k) for k in range(64)]
        return mail[c, 0:1, :] + col_times(k_t, gaps), later

    def back_step(n, carry):
        state, damp_next = carry
        c = 31 - n
        return back(c, state, damp_next)[0], mail[c, 4:5, :]

    zero = jnp.zeros((1, S), F32)
    state, damp_next = lax.fori_loop(0, 31 - tm, back_step, (zero, zero))
    state, later = back(tm, state, damp_next)
    kept[0:1, :] = state
    kept[1:2, :] = mail[tm, 1:2, :] + to_row(later)
    smooth_out[...] = kept[0:2, own_cols]
    filt_out[...] = mail[tm, 0:2, own_cols]

    def drain_mail(n, carry):
        wait_mail(n)
        return carry

    lax.fori_loop(0, tm, drain_mail, 0)
    for drain in drains:
        drain()


def hand_out(filt, smooth, filt_out, smooth_out):
    filt_out[...] = filt[...]
    smooth_out[...] = smooth[...]


def local(records, obs_values, block_day, block_count, propagator_matrix, analysis_cov, unattenuated_multiplier,
          damping, prior_mean):
    vmem = pl.BlockSpec(memory_space=pltpu.VMEM)
    hbm = pl.BlockSpec(memory_space=pl.ANY)
    smem = pl.BlockSpec(memory_space=pltpu.SMEM)
    dma = pltpu.SemaphoreType.DMA
    results = pl.pallas_call(
        kernel,
        out_shape=(jax.ShapeDtypeStruct((2, 128), F32), jax.ShapeDtypeStruct((2, 128), F32)),
        in_specs=[hbm, vmem, smem, smem] + [hbm] * 3 + [vmem] * 2,
        out_specs=(vmem, vmem),
        scratch_shapes=[
            pltpu.VMEM((16, 256, S), BF16),
            pltpu.VMEM((32, 16, 128), BF16),
            pltpu.VMEM((1040, 256), BF16),
            pltpu.VMEM((1040, S), F32),
            pltpu.VMEM((2, 128, 640), F32),
            pltpu.VMEM((2, 128, 640), F32),
            pltpu.VMEM((2, 128, 640), F32),
            pltpu.VMEM((2, 128, 640), F32),
            pltpu.VMEM((2, 128, 640), F32),
            pltpu.VMEM((3, 8, S), F32),
            pltpu.VMEM((2, S, S), F32),
            pltpu.VMEM((136, S), F32),
            pltpu.VMEM((128, S), F32),
            pltpu.VMEM((S, 128), F32),
            pltpu.VMEM((8, S), F32),
            pltpu.VMEM((8, S, S), F32),
            pltpu.VMEM((8, 8, S), F32),
            pltpu.VMEM((S, S), F32),
            pltpu.VMEM((S, S), F32),
            pltpu.VMEM((8, S), F32),
            pltpu.VMEM((8, S), F32),
            pltpu.VMEM((8, 128), F32),
            pltpu.VMEM((4, 8, 128), F32),
            pltpu.VMEM((8, S), F32),
            pltpu.VMEM((8, S), F32),
            pltpu.VMEM((8, 8, S), F32),
            pltpu.VMEM((8, S), F32),
            pltpu.VMEM((8, S), F32),
            pltpu.VMEM((32, 8, S), F32),
            pltpu.VMEM((8, S), F32),
            pltpu.VMEM((32, 2, S, 128), F32),
            pltpu.VMEM((2, S, 128), F32),
            pltpu.VMEM((4, S, 128), F32),
            dma((32,)), dma((32,)), dma((32,)), dma((32,)),
            dma((4,)), dma((4,)), dma((1,)), dma((1,)), dma((1,)), dma((4,)),
            dma((6,)), dma((6,)), dma((3,)), dma((3,)), dma((4,)), dma((4,)), dma((4,)), dma((4,)),
            dma((1,)), dma((32,)), dma((1,)), dma((8,)), dma((1,)), dma((1,)),
            dma((32,)), dma((1,)), dma((32,)), dma((32,)), dma,
            pltpu.VMEM((S, S), F32), pltpu.VMEM((S, S), F32), pltpu.VMEM((128, S), F32), dma((3,)),
            pltpu.VMEM((32, 16, 128), BF16),
            pltpu.VMEM((32, 128), F32),
            dma((4,)), dma((4,)), dma((8,)),
            pltpu.VMEM((2, S, S), BF16), pltpu.VMEM((2, S, S), BF16),
        ],
        compiler_params=pltpu.CompilerParams(collective_id=0, has_side_effects=True, vmem_limit_bytes=56 << 20),
        cost_estimate=pl.CostEstimate(flops=10**10, bytes_accessed=10**8, transcendentals=0),
    )(records, obs_values.reshape(32, 128), block_day, block_count, propagator_matrix, analysis_cov, unattenuated_multiplier, damping, prior_mean.reshape(1, 128))
    return pl.pallas_call(
        hand_out,
        out_shape=(jax.ShapeDtypeStruct((2, 128), F32), jax.ShapeDtypeStruct((2, 128), F32)),
        in_specs=[vmem, vmem],
        out_specs=(vmem, vmem),
    )(*results)


def solution(mesh):
    return jax.shard_map(
        local,
        mesh=mesh,
        in_specs=(
            P(("tm", "obs"), None),
            P(("tm", "obs")),
            P(("tm", "obs")),
            P(("tm", "obs")),
            P(),
            P(),
            P("obs", None),
            P("tm", None),
            P("obs"),
        ),
        out_specs=(P("tm", "obs"), P("tm", "obs")),
        check_vma=False,
    )
```
